32 devices in a mesh: groups: 2 (over x), ctx: 8 (over z, y), exp: 2 (over core).
Axes of the slice: x: 2, y: 2, z: 4, core: 2. Of those that a mesh axis runs over, the one named last changes fastest.
Arguments:
- x_in: bfloat16 [4096, 2048], P(('groups', 'ctx'), 'exp'), parts along dimension 0, may hold values from -6 to 6
- bc_in: bfloat16 [4096, 2, 512], P(('groups', 'ctx'), None, 'exp'), parts along dimension 0, may hold values from -6 to 6
- z_in: bfloat16 [4096, 2048], P(('groups', 'ctx'), 'exp'), parts along dimension 0, may hold values from -6 to 6
- time_step: float32 [4096, 32], P(('groups', 'ctx'), 'exp'), parts along dimension 0, may hold values from 0.002 to 0.02
- decay_log: float32 [4096, 32], P(('groups', 'ctx'), 'exp'), parts along dimension 0, may hold values from -1 to 0
- conv_inner: bfloat16 [4, 2048], P(None, 'exp'), may hold values from -3 to 3
- conv_bc: bfloat16 [4, 2, 512], P(None, None, 'exp'), may hold values from -3 to 3
- skip_gain: float32 [32], P('exp'), may hold values from 0.5 to 1.5
- start_state: bfloat16 [64, 64, 128], P(('groups', 'exp')), parts along dimension 0, may hold values from -3 to 3
- norm_gain: bfloat16 [2048], P('exp'), may hold values from 0.099609375 to 1.8984375
- out_proj: bfloat16 [2048, 2688], P('exp', 'ctx'), may hold values from -0.125 to 0.125
- residual: bfloat16 [4096, 2688], P(('groups', 'ctx', 'exp')), parts along dimension 0, may hold values from -40 to 40
- moe_gain: bfloat16 [2688], replicated, may hold values from 0.099609375 to 1.8984375
- routes: int32 [4096, 6], P(('groups', 'ctx', 'exp')), parts along dimension 0, may hold values from 0 to 15, all different within a row; in each aligned block of 128 rows (0 to 127, 128 to 255, ...) at most 64 rows name the same one
- gate_weight: float32 [4096, 6], P(('groups', 'ctx', 'exp')), parts along dimension 0, may hold values from 0.1 to 0.4
- up_weight: bfloat16 [16, 2688, 928], P(('ctx', 'exp')), may hold values from -0.125 to 0.125
- down_weight: bfloat16 [16, 928, 2688], P(('ctx', 'exp')), may hold values from -0.1875 to 0.1875
Outputs:
- layer_out: bfloat16 [4096, 2688], P(('groups', 'ctx', 'exp')), parts along dimension 0
The draws below stay inside these ranges and needn't reach their ends.
There are 2 independent parts, one for each index of `groups`. The reference program is written for one: setup_inputs(seed, part) draws one part's arguments, and reference() takes and returns one part's arrays. A program takes and returns all parts, laid end to end along the dimension named above; an argument that names none is the same for every part. Nothing has to cross between parts.
Inputs may be any that keep to these rules, and one draw needn't show every extreme that they name: `routes`: each row names 6 different experts; among the rows of one device (aligned blocks of 128 rows) no expert is named more than 64 times.
All inputs are finite; a program needn't handle non-finite values.
Results may differ from the reference program's by a relative error of at most 0.0056.
Values may be sent and summed in bfloat16 or wider, within the bound.
No kernel may reach another device: no remote copies, remote signals or barrier semaphores. Data moves between devices by JAX's collectives and lax.ppermute only.
A program may use at most 128 MiB of HBM per device.

```python
import math
import jax
import jax.numpy as jnp
import numpy as np
from jax import lax

D = 2688
SCANNED_SUBSPACES = 32
HEAD_DIM = 64
STATE = 128
GROUPS = 4
KERNEL = 4
FFE = 928
TOP = 6
TOK_DEV = 128
INNER = 2048
BC_WIDTH = 512
EXPERTS = 16
SPAN_LENGTH = 2048
CAP = 64
N_CTX = 8
N_EXP = 2


def draw_decay_log(key, part):
    seed_material = jax.random.split(jax.random.fold_in(key, 11), 7)
    fast_share = 0.5
    head_pick = jax.random.uniform(seed_material[0], (SCANNED_SUBSPACES,), jnp.float32)
    fast_rate = jnp.exp(jax.random.uniform(seed_material[1], (SCANNED_SUBSPACES,), jnp.float32, math.log(1.0 / 50.0), math.log(1.0 / 30.0)))
    slow_rate = jnp.exp(jax.random.uniform(seed_material[2], (SCANNED_SUBSPACES,), jnp.float32, math.log(0.05), math.log(0.25))) / SPAN_LENGTH
    rate = jnp.where(head_pick < fast_share, fast_rate, slow_rate)
    segments = SPAN_LENGTH // 64
    segment_factor = jnp.exp(jax.random.uniform(seed_material[3], (segments, SCANNED_SUBSPACES), jnp.float32, math.log(0.5), math.log(2.0)))
    segment_factor = jnp.repeat(segment_factor, 64, axis=0)
    roughness = jax.random.uniform(seed_material[4], (SPAN_LENGTH, SCANNED_SUBSPACES), jnp.float32, 0.5, 1.5)
    typical_log_level = -rate[None, :] * segment_factor * roughness
    spike_index = jax.random.randint(seed_material[5], (2,), 0, SPAN_LENGTH)
    sequence_indices = jnp.arange(SPAN_LENGTH)
    spike_present = jnp.any(sequence_indices[:, None] == spike_index[None, :], axis=1)
    spike_log_level = jnp.log(jax.random.uniform(seed_material[6], (SPAN_LENGTH, SCANNED_SUBSPACES), jnp.float32, 0.5, 0.8))
    layer_answer = typical_log_level + jnp.where(spike_present[:, None], spike_log_level, 0.0)
    return jnp.clip(layer_answer, -1.0, 0.0).astype(jnp.float32)


def draw_residual(key, part):
    seed_material = jax.random.split(jax.random.fold_in(key, 23), 3)
    base = jnp.clip(jax.random.normal(seed_material[0], (SPAN_LENGTH, D), jnp.float32), -4.0, 4.0)
    row_scale = jnp.exp(jax.random.uniform(seed_material[1], (SPAN_LENGTH, 1), jnp.float32, math.log(0.3), math.log(3.0)))
    column_scale = jnp.exp(jax.random.uniform(seed_material[2], (1, D), jnp.float32, math.log(0.3), math.log(3.0)))
    layer_answer = base * row_scale * column_scale
    return jnp.clip(layer_answer, -40.0, 40.0).astype(jnp.bfloat16)


def steps_of(key, extent, shards, smallest, high):
    gain, own = 1.0, jax.random.fold_in(key, 6)
    for axis_at, parts in shards:
        heights = jnp.exp(jax.random.uniform(jax.random.fold_in(own, axis_at), (parts,), jnp.float32, smallest / len(shards), high / len(shards)))
        gain = gain * jnp.repeat(heights, extent[axis_at] // parts).reshape([-1 if axis == axis_at else 1 for axis in range(len(extent))])
    return gain


def assign_block(stream_key, own, number, rows, count, top, most, slope):
    order = jax.random.permutation(stream_key, count)
    heavy_load, ordinary = shares(count, rows * top, most, slope, True), shares(count, rows * top, most, slope, False)
    places = jnp.arange(count)

    def named(tallies, rotation):
        used = int((tallies > 0).sum())
        fixed = max(1, used // 4)
        passed = fixed + (places - fixed + rotation * (used - fixed)) % max(1, count - fixed)
        return jnp.zeros((count,), jnp.int32).at[order[jnp.where(places < fixed, places, passed)]].set(jnp.asarray(tallies, jnp.int32))

    tallies = jnp.where(number % 4 == 0, named(heavy_load, number // 4), named(ordinary, number - number // 4 - 1))
    mixed = jax.random.permutation(jax.random.fold_in(own, 3), count)
    donor, taker = mixed[0:count // 2 * 2:2], mixed[1:count // 2 * 2:2]
    margin = jnp.minimum(tallies[donor] - 1, most - tallies[taker]) // 2
    margin = jnp.where((donor == order[0]) | (taker == order[0]) | (tallies[taker] == 0), 0, jnp.maximum(margin, 0))
    passed = jax.random.randint(jax.random.fold_in(own, 4), (count // 2,), 0, 1 << 20) % (margin + 1)
    tallies = tallies.at[donor].add(-passed).at[taker].add(passed)
    items = jnp.searchsorted(jnp.cumsum(tallies), jnp.arange(rows * top), side="right").astype(jnp.int32)
    listing = items.reshape(top, rows).T
    listing = listing[jax.random.permutation(jax.random.fold_in(own, 1), rows)]
    rotation = jax.random.randint(jax.random.fold_in(own, 2), (rows, 1), 0, top)
    return jnp.take_along_axis(listing, (jnp.arange(top)[None, :] + rotation) % top, axis=1)


def shares(count, total, reach, lean, full):
    loads = [(1 << 20) // math.isqrt(standing ** lean) + 1 for standing in range(1, count + 1)]
    largest = reach if full else min(reach, max(-(-total // count), total * loads[0] // sum(loads)))
    least = 1 if total - largest >= count - 1 else 0
    holding, rest = [largest] + [least] * (count - 1), total - largest - least * (count - 1)
    while rest > 0:
        free = [i for i in range(1, count) if holding[i] < largest] or [i for i in range(1, count) if holding[i] < reach]
        mass, remaining = sum([loads[i] for i in free]), rest
        for i in free:
            extra = min(reach - holding[i], max(1, remaining * loads[i] // mass), rest)
            holding[i] = holding[i] + extra
            rest = rest - extra
    return np.array(holding)


def normal_values(stream_key, dims, spread, bound, cuts=(), kind=jnp.bfloat16):
    gain = steps_of(stream_key, dims, cuts, -0.22, 0.18) if cuts else 1.0
    values = jax.random.normal(stream_key, dims, jnp.float32) * spread * gain
    return jnp.minimum(jnp.maximum(values, -bound), bound).astype(kind)


def setup_inputs(seed: int = 0, part: int = 0) -> dict:
    key_list = jax.random.split(jax.random.key(seed), 18)
    part_splits = jax.random.split(jax.random.fold_in(key_list[17], part), 18)
    x_in = normal_values(part_splits[0], (SPAN_LENGTH, INNER), 1.0, 6.0, ((0, 8), (1, 2)))
    bc_in = normal_values(part_splits[1], (SPAN_LENGTH, 2, BC_WIDTH), 1.0, 6.0, ((0, 8), (2, 2)))
    z_in = normal_values(part_splits[2], (SPAN_LENGTH, INNER), 1.0, 6.0, ((0, 8), (1, 2)))
    time_step = jnp.clip(jnp.exp(math.log(0.02) - 2.30258502 * jax.random.uniform(part_splits[3], (SPAN_LENGTH, SCANNED_SUBSPACES), jnp.float32) ** steps_of(part_splits[3], (SPAN_LENGTH, SCANNED_SUBSPACES), ((0, 8), (1, 2)), -0.2, 0.2)), 0.002, 0.02)
    decay_log = draw_decay_log(jax.random.fold_in(jax.random.fold_in(key_list[17], part), 71), part)
    conv_inner = normal_values(key_list[5], (KERNEL, INNER), KERNEL ** -0.5, 3.0, ((1, 2),))
    conv_bc = normal_values(key_list[6], (KERNEL, 2, BC_WIDTH), KERNEL ** -0.5, 3.0, ((2, 2),))
    skip_gain = jnp.clip(0.5 + 1.0 * jax.random.uniform(key_list[7], (SCANNED_SUBSPACES,), jnp.float32) ** steps_of(key_list[7], (SCANNED_SUBSPACES,), ((0, 2),), -0.2, 0.2), 0.5, 1.5)
    start_state = normal_values(part_splits[8], (SCANNED_SUBSPACES, HEAD_DIM, STATE), 0.5, 3.0, ((0, 2),))
    norm_gain = jnp.clip(1.0 + 0.18 * jax.random.normal(key_list[9], (INNER,), jnp.float32), 0.099609375, 1.8984375).astype(jnp.bfloat16)
    out_proj = normal_values(key_list[10], (INNER, D), INNER ** -0.5, 0.125, ((0, 2), (1, 8)))
    residual = draw_residual(jax.random.fold_in(jax.random.fold_in(key_list[17], part), 71), part)
    moe_gain = jnp.clip(1.0 + 0.18 * jax.random.normal(key_list[12], (D,), jnp.float32), 0.099609375, 1.8984375).astype(jnp.bfloat16)
    routes_keys = jax.random.split(jax.random.fold_in(part_splits[13], 1), SPAN_LENGTH // TOK_DEV)
    routes_turns = jax.random.permutation(jax.random.fold_in(part_splits[13], 3), SPAN_LENGTH // TOK_DEV)
    routes = jax.vmap(lambda own, number: assign_block(jax.random.fold_in(part_splits[13], 2), own, number, TOK_DEV, EXPERTS, TOP, CAP, 2))(routes_keys, routes_turns).reshape((SPAN_LENGTH, TOP))
    gate_weight = jnp.clip(0.1 + 0.3 * jax.random.uniform(part_splits[14], (SPAN_LENGTH, TOP), jnp.float32) ** steps_of(part_splits[14], (SPAN_LENGTH, TOP), ((0, 16),), -0.2, 0.2), 0.1, 0.4)
    up_weight = normal_values(key_list[15], (EXPERTS, D, FFE), D ** -0.5, 0.125, ((0, 16),))
    down_weight = normal_values(key_list[16], (EXPERTS, FFE, D), FFE ** -0.5, 0.1875, ((0, 16),))
    return {"x_in": x_in, "bc_in": bc_in, "z_in": z_in, "time_step": time_step, "decay_log": decay_log, "conv_inner": conv_inner, "conv_bc": conv_bc, "skip_gain": skip_gain, "start_state": start_state, "norm_gain": norm_gain, "out_proj": out_proj, "residual": residual, "moe_gain": moe_gain, "routes": routes, "gate_weight": gate_weight, "up_weight": up_weight, "down_weight": down_weight}


EPS = 1e-05
HIGH = lax.Precision.HIGHEST

def causal_conv(sequence, taps):
    width = taps.shape[0]
    length = sequence.shape[0]
    padded = jnp.concatenate([jnp.zeros((width - 1,) + sequence.shape[1:], jnp.float32), sequence.astype(jnp.float32)], 0)
    summed = jnp.zeros(sequence.shape, jnp.float32)
    for offset in range(width):
        summed = summed + taps[offset].astype(jnp.float32) * padded[offset:offset + length]
    return jax.nn.silu(summed).astype(jnp.bfloat16)

def reference(x_in, bc_in, z_in, time_step, decay_log, conv_inner, conv_bc, skip_gain, start_state, norm_gain, out_proj, residual, moe_gain, routes, gate_weight, up_weight, down_weight):
    inner_act = causal_conv(x_in, conv_inner)
    bc_act = causal_conv(bc_in, conv_bc)
    per_group = SCANNED_SUBSPACES // GROUPS
    group_of = jnp.arange(SCANNED_SUBSPACES, dtype=jnp.int32) // per_group
    values = inner_act.astype(jnp.float32).reshape(SPAN_LENGTH, SCANNED_SUBSPACES, HEAD_DIM)
    b_heads = bc_act[:, 0].astype(jnp.float32).reshape(SPAN_LENGTH, GROUPS, STATE)[:, group_of]
    c_heads = bc_act[:, 1].astype(jnp.float32).reshape(SPAN_LENGTH, GROUPS, STATE)[:, group_of]

    def advance(state, inputs):
        log_step, step_size, value_row, b_row, c_row = inputs
        state = jnp.exp(log_step)[:, None, None] * state + (step_size[:, None] * value_row)[:, :, None] * b_row[:, None, :]
        layer_answer = jnp.einsum('hpn,hn->hp', state, c_row, precision=HIGH)
        return (state, layer_answer)
    final_state, outputs = lax.scan(advance, start_state.astype(jnp.float32), (decay_log, time_step, values, b_heads, c_heads))
    outputs = outputs + skip_gain[None, :, None] * values
    gated = outputs.reshape(SPAN_LENGTH, GROUPS, -1) * jax.nn.silu(z_in.astype(jnp.float32).reshape(SPAN_LENGTH, GROUPS, -1))
    mean_square = lax.optimization_barrier(jnp.mean(gated * gated, axis=-1, keepdims=True))
    normed = (gated * lax.rsqrt(mean_square + EPS) * norm_gain.astype(jnp.float32).reshape(GROUPS, -1)).reshape(SPAN_LENGTH, INNER).astype(jnp.bfloat16)
    mixed = jnp.dot(normed, out_proj, preferred_element_type=jnp.float32)
    hidden = (residual.astype(jnp.float32) + mixed).astype(jnp.bfloat16)
    hidden_f = hidden.astype(jnp.float32)
    expert_in = (hidden_f * lax.rsqrt(lax.optimization_barrier(jnp.mean(hidden_f * hidden_f, axis=-1, keepdims=True)) + EPS) * moe_gain.astype(jnp.float32)).astype(jnp.bfloat16)
    flat_ids = routes.reshape(-1).astype(jnp.int32)
    flat_gates = gate_weight.reshape(-1)
    assigned = SPAN_LENGTH * TOP
    buffer_len = N_CTX * N_EXP * CAP

    def one_expert(accum, expert_id):
        chosen = flat_ids == expert_id
        rank = jnp.cumsum(chosen.astype(jnp.int32)) - 1
        target = jnp.where(chosen, rank, buffer_len).astype(jnp.int32)
        picked = jnp.zeros((buffer_len + 1,), jnp.int32).at[target].set(jnp.arange(assigned, dtype=jnp.int32))[:buffer_len]
        count = jnp.sum(chosen.astype(jnp.int32))
        token_ids = picked // TOP
        inputs_rows = expert_in[token_ids]
        inner = jnp.dot(inputs_rows, up_weight[expert_id], preferred_element_type=jnp.float32)
        inner = jnp.square(jax.nn.relu(inner)).astype(jnp.bfloat16)
        layer_answer = jnp.dot(inner, down_weight[expert_id], preferred_element_type=jnp.float32).astype(jnp.bfloat16)
        valid = jnp.arange(buffer_len, dtype=jnp.int32) < count
        weights = jnp.where(valid, flat_gates[picked], jnp.zeros((), flat_gates.dtype))
        accum = accum.at[token_ids].add(weights[:, None] * layer_answer.astype(jnp.float32))
        return (accum, count)
    accum, counts = lax.scan(one_expert, jnp.zeros((SPAN_LENGTH, D), jnp.float32), jnp.arange(EXPERTS, dtype=jnp.int32))
    return (hidden_f + accum).astype(jnp.bfloat16)
```

```python
import functools

import jax
import jax.numpy as jnp
from jax import lax
from jax.experimental import pallas as pl
from jax.experimental.pallas import tpu as pltpu
from jax.sharding import PartitionSpec as P

HEAD_DIM = 64
STATE = 128
KERNEL = 4


EPS = 1e-05
HIGH = lax.Precision.HIGHEST
BF16 = jnp.bfloat16
F32 = jnp.float32


def from_behind(array, axis, by):
    count = lax.axis_size(axis)
    pairs = [(i, i + by) for i in range(count) if 0 <= i + by < count]
    return lax.ppermute(array, axis, pairs)


def entering_state(block_log, end_state, start_state):
    count, index = lax.axis_size("ctx"), lax.axis_index("ctx")
    logs = lax.all_gather(block_log, "ctx")
    earlier = (jnp.arange(count) < index).astype(F32)[:, None, None]
    masked = logs * earlier
    after = jnp.flip(jnp.cumsum(jnp.flip(masked, 0), axis=0), 0) - masked
    whole = jnp.sum(masked, axis=0)

    def spread(coefficient):
        return jnp.exp(coefficient)[..., None, None]

    partner = lax.ppermute(
        end_state.astype(BF16), "ctx", [(i, i ^ 1) for i in range(count)]
    ).astype(F32)
    odd = index % 2
    first_log = jnp.where(odd == 1, block_log, lax.dynamic_index_in_dim(logs, index ^ 1, 0, False))
    pair = jnp.where(
        odd == 1,
        spread(first_log) * partner + end_state,
        spread(first_log) * end_state + partner,
    ).astype(BF16)
    entering = spread(whole) * start_state + jnp.where(odd == 1, partner, 0.0)
    half = count // 2

    def after_pair(back):
        place = jnp.maximum((index // 2 - back) * 2 + 1, 0)
        return lax.dynamic_index_in_dim(after, place, 0, False)

    if half <= 4:
        for back in range(half - 1, 0, -1):
            entering = entering + spread(after_pair(back)) * from_behind(
                pair, "ctx", 2 * back
            ).astype(F32)
        return entering
    window = from_behind(pair, "ctx", 2).astype(F32)
    to_start = jnp.where(odd == 1, lax.dynamic_index_in_dim(logs, index ^ 1, 0, False), 0.0)
    back = 1
    while back < half - 1:
        step_log = after_pair(back + 1) - to_start
        window = window + spread(step_log) * from_behind(
            window.astype(BF16), "ctx", 2 * back
        ).astype(F32)
        back *= 2
    return entering + spread(to_start) * window


def causal_conv(sequence, previous, taps):
    length = sequence.shape[0]
    padded = jnp.concatenate([previous, sequence], 0).astype(F32)
    summed = jnp.zeros(sequence.shape, F32)
    for offset in range(taps.shape[0]):
        summed = summed + taps[offset].astype(F32) * padded[offset : offset + length]
    return jax.nn.silu(summed).astype(BF16)


def expert_kernel(cap, tok_rows, pairs, slot_ref, gate_ref, x_ref, up_ref, down_ref, out_ref, sel_ref, ans_ref):
    rows = 2 * cap
    toks = 2 * tok_rows
    def one_hot(i):
        slots = slot_ref[0, :, i * toks : (i + 1) * toks]
        place = lax.broadcasted_iota(jnp.int32, (rows, toks), 0)
        return (place == slots).astype(F32).astype(BF16)

    for i in range(pairs):
        sel_ref[i * rows : (i + 1) * rows, :] = jnp.dot(
            one_hot(i), x_ref[i * toks : (i + 1) * toks, :], preferred_element_type=F32
        ).astype(BF16)
    inner = jnp.dot(sel_ref[...], up_ref[0], preferred_element_type=F32)
    inner = jnp.square(jnp.maximum(inner, 0.0)).astype(BF16)
    ans_ref[...] = jnp.dot(inner, down_ref[0], preferred_element_type=F32).astype(BF16)
    for i in range(pairs):
        spread = lax.dot_general(
            one_hot(i),
            ans_ref[i * rows : (i + 1) * rows, :],
            (((0,), (0,)), ((), ())),
            preferred_element_type=F32,
        )
        out_ref[i * toks : (i + 1) * toks, :] = (
            spread * gate_ref[i * toks : (i + 1) * toks, :]
        ).astype(BF16)


def run_expert(tokens, slots, gates, up_weight, down_weight, cap):
    sources, tok_rows = slots.shape
    width, hidden = up_weight.shape[1:]
    pairs = 2 if cap >= 64 else 4
    step = 2 * pairs
    offset = (jnp.arange(sources, dtype=jnp.int32) % 2 * cap)[:, None]
    slots = jnp.where(slots >= 0, slots + offset, -1).reshape(sources // step, 1, step * tok_rows)
    total = sources * tok_rows
    block = step * tok_rows
    return pl.pallas_call(
        functools.partial(expert_kernel, cap, tok_rows, pairs),
        out_shape=jax.ShapeDtypeStruct((total, width), BF16),
        grid=(sources // step,),
        in_specs=[
            pl.BlockSpec((1, 1, block), lambda i: (i, 0, 0)),
            pl.BlockSpec((block, 1), lambda i: (i, 0)),
            pl.BlockSpec((block, width), lambda i: (i, 0)),
            pl.BlockSpec((1, width, hidden), lambda i: (0, 0, 0), pipeline_mode=pl.Buffered(1)),
            pl.BlockSpec((1, hidden, width), lambda i: (0, 0, 0), pipeline_mode=pl.Buffered(1)),
        ],
        out_specs=pl.BlockSpec((block, width), lambda i: (i, 0)),
        scratch_shapes=[
            pltpu.VMEM((step * cap, width), BF16),
            pltpu.VMEM((step * cap, width), BF16),
        ],
        compiler_params=pltpu.CompilerParams(
            dimension_semantics=("arbitrary",), vmem_limit_bytes=56 << 20
        ),
        cost_estimate=pl.CostEstimate(
            flops=4 * sources * cap * width * hidden,
            bytes_accessed=4 * total * width + 4 * width * hidden,
            transcendentals=0,
        ),
    )(slots, gates.reshape(total, 1), tokens, up_weight, down_weight)


def per_device(
    x_in,
    bc_in,
    z_in,
    time_step,
    decay_log,
    conv_inner,
    conv_bc,
    skip_gain,
    start_state,
    norm_gain,
    out_proj,
    residual,
    moe_gain,
    routes,
    gate_weight,
    up_weight,
    down_weight,
):
    ctx_count = lax.axis_size("ctx")
    exp_count = lax.axis_size("exp")
    exp_index = lax.axis_index("exp")
    block_len = x_in.shape[0]
    local_heads = time_step.shape[1]
    local_groups = bc_in.shape[2] // STATE
    per_group = local_heads // local_groups
    rim_rows = KERNEL - 1
    proj = lax.all_gather(out_proj.T, "ctx", axis=0, tiled=True)

    tok_rows = routes.shape[0]
    top_count = routes.shape[1]
    experts = ctx_count * exp_count * up_weight.shape[0]
    capacity = max(2, 4 * tok_rows * top_count // (3 * experts))
    chosen = routes[:, :, None] == jnp.arange(experts, dtype=jnp.int32)[None, None, :]
    dense_gate = jnp.sum(jnp.where(chosen, gate_weight[:, :, None], 0.0), axis=1)
    all_gates = lax.all_gather(dense_gate.T, ("ctx", "exp"), axis=0)
    me = lax.axis_index("ctx") * exp_count + exp_index
    gates = lax.dynamic_index_in_dim(all_gates, me, 1, False)
    member = gates > 0.0
    slots = jnp.where(member, jnp.cumsum(member.astype(jnp.int32), axis=1) - 1, -1)

    prev_inner, prev_bc = from_behind(
        (x_in[block_len - rim_rows :], bc_in[block_len - rim_rows :]), "ctx", 1
    )
    inner_act = causal_conv(x_in, prev_inner, conv_inner)
    bc_act = causal_conv(bc_in, prev_bc, conv_bc)
    values = inner_act.astype(F32).reshape(block_len, local_groups, per_group, HEAD_DIM)
    b_rows = bc_act[:, 0].astype(F32).reshape(block_len, local_groups, STATE)
    c_rows = bc_act[:, 1].astype(F32).reshape(block_len, local_groups, STATE)
    log_steps = decay_log.reshape(block_len, local_groups, per_group)
    step_sizes = time_step.reshape(block_len, local_groups, per_group)
    cumulative = jnp.cumsum(log_steps, axis=0)
    block_log = cumulative[block_len - 1]
    to_end = jnp.exp(block_log[None] - cumulative) * step_sizes
    end_state = jnp.einsum("tgrp,tgn->grpn", to_end[..., None] * values, b_rows, precision=HIGH)
    entering = entering_state(
        block_log,
        end_state,
        start_state.astype(F32).reshape(local_groups, per_group, HEAD_DIM, STATE),
    )
    carried = jnp.exp(cumulative)[..., None] * jnp.einsum(
        "tgn,grpn->tgrp", c_rows, entering, precision=HIGH
    )
    scores = jnp.einsum("tgn,sgn->tsg", c_rows, b_rows, precision=HIGH)
    position = jnp.arange(block_len)
    causal = (position[:, None] >= position[None, :])[:, :, None, None]
    spread_log = cumulative[:, None] - cumulative[None, :]
    decay_table = jnp.where(causal, jnp.exp(jnp.where(causal, spread_log, 0.0)), 0.0)
    mix_table = decay_table * step_sizes[None] * scores[..., None]
    local_part = jnp.einsum("tsgr,sgrp->tgrp", mix_table, values, precision=HIGH)
    outputs = (
        carried + local_part + skip_gain.reshape(local_groups, per_group)[None, :, :, None] * values
    )
    gated = outputs.reshape(block_len, local_groups, -1) * jax.nn.silu(
        z_in.astype(F32).reshape(block_len, local_groups, -1)
    )
    mean_square = jnp.mean(gated * gated, axis=-1, keepdims=True)
    normed = (
        (gated * lax.rsqrt(mean_square + EPS) * norm_gain.astype(F32).reshape(local_groups, -1))
        .reshape(block_len, -1)
        .astype(BF16)
    )

    def projected(part):
        rows = lax.dynamic_slice_in_dim(normed, part * tok_rows, tok_rows, 0)
        return lax.dot_general(rows, proj, (((1,), (1,)), ((), ())), preferred_element_type=F32)

    theirs = lax.ppermute(projected(1 - exp_index), "exp", [(0, 1), (1, 0)])
    mixed = projected(exp_index) + theirs
    hidden_f = (residual.astype(F32) + mixed).astype(BF16).astype(F32)
    expert_in = (
        hidden_f
        * lax.rsqrt(jnp.mean(hidden_f * hidden_f, axis=-1, keepdims=True) + EPS)
        * moe_gain.astype(F32)
    ).astype(BF16)
    tokens = lax.all_gather(expert_in, ("ctx", "exp"), axis=0, tiled=True)
    answers = run_expert(tokens, slots, gates, up_weight, down_weight, capacity)
    combined = lax.psum_scatter(answers, ("ctx", "exp"), scatter_dimension=0, tiled=True)
    return (hidden_f + combined.astype(F32)).astype(BF16)


def solution(mesh):
    in_specs = (
        P(("groups", "ctx"), "exp"),
        P(("groups", "ctx"), None, "exp"),
        P(("groups", "ctx"), "exp"),
        P(("groups", "ctx"), "exp"),
        P(("groups", "ctx"), "exp"),
        P(None, "exp"),
        P(None, None, "exp"),
        P("exp"),
        P(("groups", "exp"), None, None),
        P("exp"),
        P("exp", "ctx"),
        P(("groups", "ctx", "exp"), None),
        P(),
        P(("groups", "ctx", "exp"), None),
        P(("groups", "ctx", "exp"), None),
        P(("ctx", "exp"), None, None),
        P(("ctx", "exp"), None, None),
    )
    out_specs = P(("groups", "ctx", "exp"), None)
    return jax.shard_map(
        per_device, mesh=mesh, in_specs=in_specs, out_specs=out_specs, check_vma=False
    )
```

```python
import functools

import jax
import jax.numpy as jnp
from jax import lax
from jax.experimental import pallas as pl
from jax.experimental.pallas import tpu as pltpu
from jax.sharding import PartitionSpec as P

HEAD_DIM = 64
STATE = 128
KERNEL = 4


EPS = 1e-05
HIGH = lax.Precision.HIGHEST
BF16 = jnp.bfloat16
F32 = jnp.float32


def from_behind(array, axis, by):
    count = lax.axis_size(axis)
    pairs = [(i, i + by) for i in range(count) if 0 <= i + by < count]
    return lax.ppermute(array, axis, pairs)


def entering_state(block_log, logs, end_state, start_state):
    count, index = lax.axis_size("ctx"), lax.axis_index("ctx")
    earlier = (jnp.arange(count) < index).astype(F32)[:, None, None]
    masked = logs * earlier
    after = jnp.flip(jnp.cumsum(jnp.flip(masked, 0), axis=0), 0) - masked
    whole = jnp.sum(masked, axis=0)

    def spread(coefficient):
        return jnp.exp(coefficient)[..., None, None]

    partner = lax.ppermute(
        end_state.astype(BF16), "ctx", [(i, i ^ 1) for i in range(count)]
    ).astype(F32)
    odd = index % 2
    first_log = jnp.where(odd == 1, block_log, lax.dynamic_index_in_dim(logs, index ^ 1, 0, False))
    pair = jnp.where(
        odd == 1,
        spread(first_log) * partner + end_state,
        spread(first_log) * end_state + partner,
    ).astype(BF16)
    entering = spread(whole) * start_state + jnp.where(odd == 1, partner, 0.0)
    half = count // 2

    def after_pair(back):
        place = jnp.maximum((index // 2 - back) * 2 + 1, 0)
        return lax.dynamic_index_in_dim(after, place, 0, False)

    if half <= 4:
        for back in range(half - 1, 0, -1):
            entering = entering + spread(after_pair(back)) * from_behind(
                pair, "ctx", 2 * back
            ).astype(F32)
        return entering
    window = from_behind(pair, "ctx", 2).astype(F32)
    to_start = jnp.where(odd == 1, lax.dynamic_index_in_dim(logs, index ^ 1, 0, False), 0.0)
    back = 1
    while back < half - 1:
        step_log = after_pair(back + 1) - to_start
        window = window + spread(step_log) * from_behind(
            window.astype(BF16), "ctx", 2 * back
        ).astype(F32)
        back *= 2
    return entering + spread(to_start) * window


def causal_conv(sequence, previous, taps):
    length = sequence.shape[0]
    padded = jnp.concatenate([previous, sequence], 0).astype(F32)
    summed = jnp.zeros(sequence.shape, F32)
    for offset in range(taps.shape[0]):
        summed = summed + taps[offset].astype(F32) * padded[offset : offset + length]
    return jax.nn.silu(summed).astype(BF16)


def expert_kernel(cap, tok_rows, pairs, slot_ref, gate_ref, x_ref, up_ref, down_ref, out_ref, sel_ref, ans_ref):
    rows = 2 * cap
    toks = 2 * tok_rows
    def one_hot(i):
        slots = slot_ref[0, :, i * toks : (i + 1) * toks]
        place = lax.broadcasted_iota(jnp.int32, (rows, toks), 0)
        return (place == slots).astype(F32).astype(BF16)

    for i in range(pairs):
        sel_ref[i * rows : (i + 1) * rows, :] = jnp.dot(
            one_hot(i), x_ref[i * toks : (i + 1) * toks, :], preferred_element_type=F32
        ).astype(BF16)
    inner = jnp.dot(sel_ref[...], up_ref[0], preferred_element_type=F32)
    inner = jnp.square(jnp.maximum(inner, 0.0)).astype(BF16)
    ans_ref[...] = jnp.dot(inner, down_ref[0], preferred_element_type=F32).astype(BF16)
    for i in range(pairs):
        spread = lax.dot_general(
            one_hot(i),
            ans_ref[i * rows : (i + 1) * rows, :],
            (((0,), (0,)), ((), ())),
            preferred_element_type=F32,
        )
        out_ref[i * toks : (i + 1) * toks, :] = (
            spread * gate_ref[i * toks : (i + 1) * toks, :]
        ).astype(BF16)


def run_expert(tokens, slots, gates, up_weight, down_weight, cap):
    sources, tok_rows = slots.shape
    width, hidden = up_weight.shape[1:]
    pairs = 2 if cap >= 64 else 4
    step = 2 * pairs
    offset = (jnp.arange(sources, dtype=jnp.int32) % 2 * cap)[:, None]
    slots = jnp.where(slots >= 0, slots + offset, -1).reshape(sources // step, 1, step * tok_rows)
    total = sources * tok_rows
    block = step * tok_rows
    return pl.pallas_call(
        functools.partial(expert_kernel, cap, tok_rows, pairs),
        out_shape=jax.ShapeDtypeStruct((total, width), BF16),
        grid=(sources // step,),
        in_specs=[
            pl.BlockSpec((1, 1, block), lambda i: (i, 0, 0)),
            pl.BlockSpec((block, 1), lambda i: (i, 0)),
            pl.BlockSpec((block, width), lambda i: (i, 0)),
            pl.BlockSpec((1, width, hidden), lambda i: (0, 0, 0), pipeline_mode=pl.Buffered(1)),
            pl.BlockSpec((1, hidden, width), lambda i: (0, 0, 0), pipeline_mode=pl.Buffered(1)),
        ],
        out_specs=pl.BlockSpec((block, width), lambda i: (i, 0)),
        scratch_shapes=[
            pltpu.VMEM((step * cap, width), BF16),
            pltpu.VMEM((step * cap, width), BF16),
        ],
        compiler_params=pltpu.CompilerParams(
            dimension_semantics=("arbitrary",), vmem_limit_bytes=56 << 20
        ),
        cost_estimate=pl.CostEstimate(
            flops=4 * sources * cap * width * hidden,
            bytes_accessed=4 * total * width + 4 * width * hidden,
            transcendentals=0,
        ),
    )(slots, gates.reshape(total, 1), tokens, up_weight, down_weight)


STEP = 4


def pick(cap, slots):
    place = lax.broadcasted_iota(jnp.int32, (cap, slots.shape[1]), 0)
    return (place == slots).astype(F32).astype(BF16)


def dot_t(a, b):
    return lax.dot_general(a, b, (((1,), (1,)), ((), ())), preferred_element_type=F32)


def spread_rows(one_hot, answers, gate):
    rows = lax.dot_general(
        one_hot, answers, (((0,), (0,)), ((), ())), preferred_element_type=F32
    )
    return (rows * gate).astype(BF16)


def first_up_kernel(cap, toks, sources, *refs):
    slot_ref, up_hbm = refs[:2]
    blocks = refs[2 : 2 + sources]
    out_ref, x_ref, up_ref, sel_ref, sems, up_sem = refs[2 + sources :]
    width = x_ref.shape[2]
    i = pl.program_id(0)

    def block_copy(k):
        return pltpu.make_async_copy(blocks[k], x_ref.at[k], sems.at[k])

    up_copy = pltpu.make_async_copy(up_hbm.at[0, :, pl.ds(0, width)], up_ref, up_sem)

    @pl.when(i == 0)
    def _():
        for k in range(sources):
            block_copy(k).start()
        up_copy.start()

    for step in range(sources // STEP):
        @pl.when(i == step)
        def _():
            for k in range(step * STEP, (step + 1) * STEP):
                block_copy(k).wait()
            if step == 0:
                up_copy.wait()

    for j in range(STEP):
        one_hot = pick(cap, slot_ref[0, :, j * toks : (j + 1) * toks])
        sel_ref[j * cap : (j + 1) * cap, :] = jnp.dot(
            one_hot, x_ref[i * STEP + j], preferred_element_type=F32
        ).astype(BF16)
    out_ref[...] = dot_t(sel_ref[...], up_ref[...])


def second_kernel(
    cap, toks, split, order_ref, slot_ref, gate_ref, part_ref, up_hbm, down_hbm, *refs
):
    blocks = refs[:STEP]
    inner_ref, out_hbm, up_ref, down_ref, sel_ref, ans_ref, buf_ref, w_sems, sems = refs[STEP:]
    width = up_ref.shape[1]
    i = pl.program_id(0)
    last = pl.num_programs(0) - 1
    now = lax.rem(i, 2)
    up_copy = pltpu.make_async_copy(up_hbm.at[0, :, pl.ds(split, width)], up_ref, w_sems.at[0])
    down_copy = pltpu.make_async_copy(
        down_hbm.at[0, :, pl.ds(split, width)], down_ref, w_sems.at[1]
    )

    @pl.when(i == 0)
    def _():
        up_copy.start()
        down_copy.start()

    def out_copy(step, slot, j):
        source = order_ref[step * STEP + j]
        return pltpu.make_async_copy(
            buf_ref.at[slot, j],
            out_hbm.at[pl.ds(pl.multiple_of(source * toks, toks), toks), :],
            sems.at[slot, j],
        )

    one_hots = []
    for j in range(STEP):
        one_hots.append(pick(cap, slot_ref[0, :, j * toks : (j + 1) * toks]))
        sel_ref[j * cap : (j + 1) * cap, :] = jnp.dot(
            one_hots[j], blocks[j][...], preferred_element_type=F32
        ).astype(BF16)

    @pl.when(i == 0)
    def _():
        up_copy.wait()

    inner = part_ref[...] + dot_t(sel_ref[...], up_ref[...])
    inner = jnp.square(jnp.maximum(inner, 0.0)).astype(BF16)
    inner_ref[...] = inner

    @pl.when(i == 0)
    def _():
        down_copy.wait()

    ans_ref[...] = jnp.dot(inner, down_ref[...], preferred_element_type=F32).astype(BF16)

    @pl.when(i >= 2)
    def _():
        for j in range(STEP):
            out_copy(i - 2, now, j).wait()

    for j in range(STEP):
        buf_ref[now, j] = spread_rows(
            one_hots[j],
            ans_ref[j * cap : (j + 1) * cap, :],
            gate_ref[j * toks : (j + 1) * toks, :],
        )
        out_copy(i, now, j).start()

    @pl.when(i == last)
    def _():
        for j in range(STEP):
            out_copy(i - 1, 1 - now, j).wait()
            out_copy(i, now, j).wait()


def third_kernel(cap, toks, half, slot_ref, gate_ref, inner_ref, down_ref, own_ref, other_ref, ans_ref):
    ans_ref[...] = jnp.dot(inner_ref[...], down_ref[0], preferred_element_type=F32).astype(BF16)

    def put(out_ref):
        for j in range(STEP):
            out_ref[j * toks : (j + 1) * toks, :] = spread_rows(
                pick(cap, slot_ref[0, :, j * toks : (j + 1) * toks]),
                ans_ref[j * cap : (j + 1) * cap, :],
                gate_ref[j * toks : (j + 1) * toks, :],
            )

    i = pl.program_id(0)
    pl.when(i < half)(lambda: put(own_ref))
    pl.when(i >= half)(lambda: put(other_ref))


def kernel_params():
    return pltpu.CompilerParams(dimension_semantics=("arbitrary",), vmem_limit_bytes=56 << 20)


def first_up(blocks, slots, up_t, cap):
    sources, toks = len(blocks), blocks[0].shape[0]
    width, hidden = blocks[0].shape[1], up_t.shape[1]
    steps = sources // STEP
    return pl.pallas_call(
        functools.partial(first_up_kernel, cap, toks, sources),
        out_shape=jax.ShapeDtypeStruct((sources * cap, hidden), F32),
        grid=(steps,),
        in_specs=[pl.BlockSpec((1, 1, STEP * toks), lambda i: (i, 0, 0))]
        + [pl.BlockSpec(memory_space=pl.ANY)] * (1 + sources),
        out_specs=pl.BlockSpec((STEP * cap, hidden), lambda i: (i, 0)),
        scratch_shapes=[
            pltpu.VMEM((sources, toks, width), BF16),
            pltpu.VMEM((hidden, width), BF16),
            pltpu.VMEM((STEP * cap, width), BF16),
            pltpu.SemaphoreType.DMA((sources,)),
            pltpu.SemaphoreType.DMA,
        ],
        compiler_params=kernel_params(),
        cost_estimate=pl.CostEstimate(
            flops=2 * sources * cap * width * hidden,
            bytes_accessed=2 * width * (sources * toks + hidden) + 4 * sources * cap * hidden,
            transcendentals=0,
        ),
    )(slots.reshape(steps, 1, STEP * toks), up_t, *blocks)


def second_part(tokens, part, order, slots, gates, up_t, down, split, cap):
    sources, toks = slots.shape
    width, hidden = tokens.shape[1], up_t.shape[1]
    steps = sources // STEP

    def source_spec(j):
        return pl.BlockSpec((toks, width), lambda i, order: (order[i * STEP + j], 0))

    return pl.pallas_call(
        functools.partial(second_kernel, cap, toks, split),
        out_shape=(
            jax.ShapeDtypeStruct((sources * cap, hidden), BF16),
            jax.ShapeDtypeStruct((sources * toks, width), BF16),
        ),
        grid_spec=pltpu.PrefetchScalarGridSpec(
            num_scalar_prefetch=1,
            grid=(steps,),
            in_specs=[
                pl.BlockSpec((1, 1, STEP * toks), lambda i, order: (i, 0, 0)),
                pl.BlockSpec((STEP * toks, 1), lambda i, order: (i, 0)),
                pl.BlockSpec((STEP * cap, hidden), lambda i, order: (i, 0)),
                pl.BlockSpec(memory_space=pl.ANY),
                pl.BlockSpec(memory_space=pl.ANY),
            ]
            + [source_spec(j) for j in range(STEP)],
            out_specs=[
                pl.BlockSpec((STEP * cap, hidden), lambda i, order: (i, 0)),
                pl.BlockSpec(memory_space=pl.ANY),
            ],
            scratch_shapes=[
                pltpu.VMEM((hidden, width), BF16),
                pltpu.VMEM((hidden, width), BF16),
                pltpu.VMEM((STEP * cap, width), BF16),
                pltpu.VMEM((STEP * cap, width), BF16),
                pltpu.VMEM((2, STEP, toks, width), BF16),
                pltpu.SemaphoreType.DMA((2,)),
                pltpu.SemaphoreType.DMA((2, STEP)),
            ],
        ),
        compiler_params=kernel_params(),
        cost_estimate=pl.CostEstimate(
            flops=4 * sources * cap * width * hidden,
            bytes_accessed=4 * width * (sources * toks + hidden) + 6 * sources * cap * hidden,
            transcendentals=0,
        ),
    )(
        order,
        slots.reshape(steps, 1, STEP * toks),
        gates,
        part,
        up_t,
        down,
        *([tokens] * STEP),
    )


def third_part(inner, slots, gates, down, width, cap):
    sources, toks = slots.shape
    hidden = inner.shape[1]
    steps = sources // STEP
    half = steps // 2
    shape = jax.ShapeDtypeStruct((sources * toks // 2, width), BF16)
    return pl.pallas_call(
        functools.partial(third_kernel, cap, toks, half),
        out_shape=(shape, shape),
        grid=(steps,),
        in_specs=[
            pl.BlockSpec((1, 1, STEP * toks), lambda i: (i, 0, 0)),
            pl.BlockSpec((STEP * toks, 1), lambda i: (i, 0)),
            pl.BlockSpec((STEP * cap, hidden), lambda i: (i, 0)),
            pl.BlockSpec((1, hidden, width), lambda i: (0, 0, 0), pipeline_mode=pl.Buffered(1)),
        ],
        out_specs=[
            pl.BlockSpec((STEP * toks, width), lambda i: (jnp.minimum(i, half - 1), 0)),
            pl.BlockSpec((STEP * toks, width), lambda i: (jnp.maximum(i - half, 0), 0)),
        ],
        scratch_shapes=[pltpu.VMEM((STEP * cap, width), BF16)],
        compiler_params=kernel_params(),
        cost_estimate=pl.CostEstimate(
            flops=2 * sources * cap * width * hidden,
            bytes_accessed=2 * width * (sources * toks + hidden) + 2 * sources * cap * hidden,
            transcendentals=0,
        ),
    )(slots.reshape(steps, 1, STEP * toks), gates, inner, down)


def swap_axis(array, axis):
    count = lax.axis_size(axis)
    return lax.ppermute(array, axis, [(i, i ^ 1) for i in range(count)])


def along_pairs(array, by):
    half = lax.axis_size("ctx") // 2
    pairs = [
        (2 * i + r, (i + by) % half * 2 + r) for i in range(half) for r in range(2)
    ]
    return lax.ppermute(array, "ctx", pairs)


def split_experts(expert_in, order, slots, gates, up_weight, down_weight, cap, split):
    half = lax.axis_size("ctx") // 2
    toks = expert_in.shape[0]
    up_t = jnp.swapaxes(up_weight, 1, 2)
    slots = slots[order]
    gates = gates[order].reshape(-1, 1)
    late = lax.all_gather(expert_in[:, split:], ("ctx", "exp"), axis=0, tiled=True)
    here = [expert_in[:, :split]]
    shifts = [half // 2] + [s for s in range(1, half) if s != half // 2]
    come = {s: along_pairs(here[0], s) for s in shifts if s}
    here += [come[s] for s in range(1, half)]
    here += [swap_axis(block, "ctx") for block in here]
    here += [swap_axis(block, "exp") for block in here]
    part = first_up(here, slots, up_t, cap)
    inner, answers = second_part(
        late, part, order, slots, gates, up_t, down_weight, split, cap
    )
    late_sum = lax.psum_scatter(answers, ("ctx", "exp"), scatter_dimension=0, tiled=True)
    own, other = third_part(inner, slots, gates, down_weight, split, cap)
    mid = half * toks
    far = own[mid:] + swap_axis(other[mid:], "exp")
    near = own[:mid] + swap_axis(other[:mid], "exp")
    total = None
    for s in shifts + [0]:
        rows = slice(s * toks, (s + 1) * toks)
        block = near[rows] + swap_axis(far[rows], "ctx")
        if s:
            block = along_pairs(block, -s)
        block = block.astype(F32)
        total = block if total is None else total + block
    return jnp.concatenate([total, late_sum.astype(F32)], axis=1)


def per_device(
    x_in,
    bc_in,
    z_in,
    time_step,
    decay_log,
    conv_inner,
    conv_bc,
    skip_gain,
    start_state,
    norm_gain,
    out_proj,
    residual,
    moe_gain,
    routes,
    gate_weight,
    up_weight,
    down_weight,
):
    ctx_count = lax.axis_size("ctx")
    exp_count = lax.axis_size("exp")
    exp_index = lax.axis_index("exp")
    block_len = x_in.shape[0]
    local_heads = time_step.shape[1]
    local_groups = bc_in.shape[2] // STATE
    per_group = local_heads // local_groups
    rim_rows = KERNEL - 1
    proj = lax.all_gather(out_proj.T, "ctx", axis=0, tiled=True)

    tok_rows = routes.shape[0]
    top_count = routes.shape[1]
    experts = ctx_count * exp_count * up_weight.shape[0]
    capacity = max(2, 4 * tok_rows * top_count // (3 * experts))
    chosen = routes[:, :, None] == jnp.arange(experts, dtype=jnp.int32)[None, None, :]
    dense_gate = jnp.sum(jnp.where(chosen, gate_weight[:, :, None], 0.0), axis=1)
    log_steps = decay_log.reshape(block_len, local_groups, per_group)
    cumulative = jnp.cumsum(log_steps, axis=0)
    block_log = cumulative[block_len - 1]
    table = jnp.concatenate(
        [dense_gate.T, jnp.pad(block_log.reshape(1, -1), ((0, 0), (0, tok_rows - local_heads)))], 0
    )
    tables = lax.all_gather(table, ("ctx", "exp"), axis=0)
    ctx_index = lax.axis_index("ctx")
    me = ctx_index * exp_count + exp_index
    gates = lax.dynamic_index_in_dim(tables, me, 1, False)
    logs = lax.dynamic_index_in_dim(
        tables[:, experts, :local_heads].reshape(ctx_count, exp_count, local_groups, per_group),
        exp_index,
        1,
        False,
    )
    member = gates > 0.0
    slots = jnp.where(member, jnp.cumsum(member.astype(jnp.int32), axis=1) - 1, -1)

    prev_inner, prev_bc = from_behind(
        (x_in[block_len - rim_rows :], bc_in[block_len - rim_rows :]), "ctx", 1
    )
    inner_act = causal_conv(x_in, prev_inner, conv_inner)
    bc_act = causal_conv(bc_in, prev_bc, conv_bc)
    values = inner_act.astype(F32).reshape(block_len, local_groups, per_group, HEAD_DIM)
    b_rows = bc_act[:, 0].astype(F32).reshape(block_len, local_groups, STATE)
    c_rows = bc_act[:, 1].astype(F32).reshape(block_len, local_groups, STATE)
    step_sizes = time_step.reshape(block_len, local_groups, per_group)
    to_end = jnp.exp(block_log[None] - cumulative) * step_sizes
    end_state = jnp.einsum("tgrp,tgn->grpn", to_end[..., None] * values, b_rows, precision=HIGH)
    entering = entering_state(
        block_log,
        logs,
        end_state,
        start_state.astype(F32).reshape(local_groups, per_group, HEAD_DIM, STATE),
    )
    carried = jnp.exp(cumulative)[..., None] * jnp.einsum(
        "tgn,grpn->tgrp", c_rows, entering, precision=HIGH
    )
    scores = jnp.einsum("tgn,sgn->tsg", c_rows, b_rows, precision=HIGH)
    position = jnp.arange(block_len)
    causal = (position[:, None] >= position[None, :])[:, :, None, None]
    spread_log = cumulative[:, None] - cumulative[None, :]
    decay_table = jnp.where(causal, jnp.exp(jnp.where(causal, spread_log, 0.0)), 0.0)
    mix_table = decay_table * step_sizes[None] * scores[..., None]
    local_part = jnp.einsum("tsgr,sgrp->tgrp", mix_table, values, precision=HIGH)
    outputs = (
        carried + local_part + skip_gain.reshape(local_groups, per_group)[None, :, :, None] * values
    )
    gated = outputs.reshape(block_len, local_groups, -1) * jax.nn.silu(
        z_in.astype(F32).reshape(block_len, local_groups, -1)
    )
    mean_square = jnp.mean(gated * gated, axis=-1, keepdims=True)
    normed = (
        (gated * lax.rsqrt(mean_square + EPS) * norm_gain.astype(F32).reshape(local_groups, -1))
        .reshape(block_len, -1)
        .astype(BF16)
    )

    def projected(part):
        rows = lax.dynamic_slice_in_dim(normed, part * tok_rows, tok_rows, 0)
        return lax.dot_general(rows, proj, (((1,), (1,)), ((), ())), preferred_element_type=F32)

    theirs = lax.ppermute(projected(1 - exp_index), "exp", [(0, 1), (1, 0)])
    mixed = projected(exp_index) + theirs
    hidden_f = (residual.astype(F32) + mixed).astype(BF16).astype(F32)
    expert_in = (
        hidden_f
        * lax.rsqrt(jnp.mean(hidden_f * hidden_f, axis=-1, keepdims=True) + EPS)
        * moe_gain.astype(F32)
    ).astype(BF16)
    half = ctx_count // 2
    if ctx_count % 2 == 0 and 1 < half <= 4 and exp_count == 2:
        place = jnp.arange(2 * ctx_count, dtype=jnp.int32)
        back = ctx_index // 2 + half - place % half
        order = back % half * 4 + (ctx_index + place // half) % 2 * 2 + (
            exp_index + place // ctx_count
        ) % 2
        split = expert_in.shape[1] // 256 * 128
        combined = split_experts(
            expert_in, order, slots, gates, up_weight, down_weight, capacity, split
        )
    else:
        tokens = lax.all_gather(expert_in, ("ctx", "exp"), axis=0, tiled=True)
        answers = run_expert(tokens, slots, gates, up_weight, down_weight, capacity)
        combined = lax.psum_scatter(answers, ("ctx", "exp"), scatter_dimension=0, tiled=True)
    return (hidden_f + combined.astype(F32)).astype(BF16)


def solution(mesh):
    in_specs = (
        P(("groups", "ctx"), "exp"),
        P(("groups", "ctx"), None, "exp"),
        P(("groups", "ctx"), "exp"),
        P(("groups", "ctx"), "exp"),
        P(("groups", "ctx"), "exp"),
        P(None, "exp"),
        P(None, None, "exp"),
        P("exp"),
        P(("groups", "exp"), None, None),
        P("exp"),
        P("exp", "ctx"),
        P(("groups", "ctx", "exp"), None),
        P(),
        P(("groups", "ctx", "exp"), None),
        P(("groups", "ctx", "exp"), None),
        P(("ctx", "exp"), None, None),
        P(("ctx", "exp"), None, None),
    )
    out_specs = P(("groups", "ctx", "exp"), None)
    return jax.shard_map(
        per_device, mesh=mesh, in_specs=in_specs, out_specs=out_specs, check_vma=False
    )
```

```python
import functools

import jax
import jax.numpy as jnp
from jax import lax
from jax.experimental import pallas as pl
from jax.experimental.pallas import tpu as pltpu
from jax.sharding import PartitionSpec as P

HEAD_DIM = 64
STATE = 128
KERNEL = 4


EPS = 1e-05
HIGH = lax.Precision.HIGHEST
BF16 = jnp.bfloat16
F32 = jnp.float32


def from_behind(array, axis, by):
    count = lax.axis_size(axis)
    pairs = [(i, i + by) for i in range(count) if 0 <= i + by < count]
    return lax.ppermute(array, axis, pairs)


def entering_state(block_log, logs, end_state, start_state):
    count, index = lax.axis_size("ctx"), lax.axis_index("ctx")
    earlier = (jnp.arange(count) < index).astype(F32)[:, None, None]
    masked = logs * earlier
    after = jnp.flip(jnp.cumsum(jnp.flip(masked, 0), axis=0), 0) - masked
    whole = jnp.sum(masked, axis=0)

    def spread(coefficient):
        return jnp.exp(coefficient)[..., None, None]

    partner = lax.ppermute(
        end_state.astype(BF16), "ctx", [(i, i ^ 1) for i in range(count)]
    ).astype(F32)
    odd = index % 2
    first_log = jnp.where(odd == 1, block_log, lax.dynamic_index_in_dim(logs, index ^ 1, 0, False))
    pair = jnp.where(
        odd == 1,
        spread(first_log) * partner + end_state,
        spread(first_log) * end_state + partner,
    ).astype(BF16)
    entering = spread(whole) * start_state + jnp.where(odd == 1, partner, 0.0)
    half = count // 2

    def after_pair(back):
        place = jnp.maximum((index // 2 - back) * 2 + 1, 0)
        return lax.dynamic_index_in_dim(after, place, 0, False)

    if half <= 4:
        for back in range(half - 1, 0, -1):
            entering = entering + spread(after_pair(back)) * from_behind(
                pair, "ctx", 2 * back
            ).astype(F32)
        return entering
    window = from_behind(pair, "ctx", 2).astype(F32)
    to_start = jnp.where(odd == 1, lax.dynamic_index_in_dim(logs, index ^ 1, 0, False), 0.0)
    back = 1
    while back < half - 1:
        step_log = after_pair(back + 1) - to_start
        window = window + spread(step_log) * from_behind(
            window.astype(BF16), "ctx", 2 * back
        ).astype(F32)
        back *= 2
    return entering + spread(to_start) * window


def causal_conv(sequence, previous, taps):
    length = sequence.shape[0]
    padded = jnp.concatenate([previous, sequence], 0).astype(F32)
    summed = jnp.zeros(sequence.shape, F32)
    for offset in range(taps.shape[0]):
        summed = summed + taps[offset].astype(F32) * padded[offset : offset + length]
    return jax.nn.silu(summed).astype(BF16)


def expert_kernel(cap, tok_rows, pairs, slot_ref, gate_ref, x_ref, up_ref, down_ref, out_ref, sel_ref, ans_ref):
    rows = 2 * cap
    toks = 2 * tok_rows
    def one_hot(i):
        slots = slot_ref[0, :, i * toks : (i + 1) * toks]
        place = lax.broadcasted_iota(jnp.int32, (rows, toks), 0)
        return (place == slots).astype(F32).astype(BF16)

    for i in range(pairs):
        sel_ref[i * rows : (i + 1) * rows, :] = jnp.dot(
            one_hot(i), x_ref[i * toks : (i + 1) * toks, :], preferred_element_type=F32
        ).astype(BF16)
    inner = jnp.dot(sel_ref[...], up_ref[0], preferred_element_type=F32)
    inner = jnp.square(jnp.maximum(inner, 0.0)).astype(BF16)
    ans_ref[...] = jnp.dot(inner, down_ref[0], preferred_element_type=F32).astype(BF16)
    for i in range(pairs):
        spread = lax.dot_general(
            one_hot(i),
            ans_ref[i * rows : (i + 1) * rows, :],
            (((0,), (0,)), ((), ())),
            preferred_element_type=F32,
        )
        out_ref[i * toks : (i + 1) * toks, :] = (
            spread * gate_ref[i * toks : (i + 1) * toks, :]
        ).astype(BF16)


def run_expert(tokens, slots, gates, up_weight, down_weight, cap):
    sources, tok_rows = slots.shape
    width, hidden = up_weight.shape[1:]
    pairs = 2 if cap >= 64 else 4
    step = 2 * pairs
    offset = (jnp.arange(sources, dtype=jnp.int32) % 2 * cap)[:, None]
    slots = jnp.where(slots >= 0, slots + offset, -1).reshape(sources // step, 1, step * tok_rows)
    total = sources * tok_rows
    block = step * tok_rows
    return pl.pallas_call(
        functools.partial(expert_kernel, cap, tok_rows, pairs),
        out_shape=jax.ShapeDtypeStruct((total, width), BF16),
        grid=(sources // step,),
        in_specs=[
            pl.BlockSpec((1, 1, block), lambda i: (i, 0, 0)),
            pl.BlockSpec((block, 1), lambda i: (i, 0)),
            pl.BlockSpec((block, width), lambda i: (i, 0)),
            pl.BlockSpec((1, width, hidden), lambda i: (0, 0, 0), pipeline_mode=pl.Buffered(1)),
            pl.BlockSpec((1, hidden, width), lambda i: (0, 0, 0), pipeline_mode=pl.Buffered(1)),
        ],
        out_specs=pl.BlockSpec((block, width), lambda i: (i, 0)),
        scratch_shapes=[
            pltpu.VMEM((step * cap, width), BF16),
            pltpu.VMEM((step * cap, width), BF16),
        ],
        compiler_params=pltpu.CompilerParams(
            dimension_semantics=("arbitrary",), vmem_limit_bytes=56 << 20
        ),
        cost_estimate=pl.CostEstimate(
            flops=4 * sources * cap * width * hidden,
            bytes_accessed=4 * total * width + 4 * width * hidden,
            transcendentals=0,
        ),
    )(slots, gates.reshape(total, 1), tokens, up_weight, down_weight)


def dot_t(a, b):
    return lax.dot_general(a, b, (((1,), (1,)), ((), ())), preferred_element_type=F32)


def dense_kernel(toks, count, gate_ref, *refs):
    blocks = refs[:count]
    up_ref, down_ref = refs[count : count + 2]
    outs = refs[count + 2 : 2 * count + 2]
    x_ref, y_ref = refs[2 * count + 2 :]
    for j in range(count):
        x_ref[j * toks : (j + 1) * toks, :] = blocks[j][...]
    size = 2 * toks

    def part(n, carry):
        rows = pl.ds(pl.multiple_of(n * size, size), size)
        inner = dot_t(x_ref[rows, :], up_ref[0])
        inner = jnp.square(jnp.maximum(inner, 0.0)).astype(BF16)
        answers = jnp.dot(inner, down_ref[0], preferred_element_type=F32)
        y_ref[rows, :] = (answers.astype(BF16).astype(F32) * gate_ref[rows, :]).astype(BF16)
        return carry

    lax.fori_loop(0, count // 2, part, 0)
    for j in range(count):
        outs[j][...] = y_ref[j * toks : (j + 1) * toks, :]


def dense_expert(blocks, gates, up_t, down):
    toks, width = blocks[0].shape
    hidden = up_t.shape[1]
    count = len(blocks)
    whole = pl.BlockSpec(memory_space=pltpu.VMEM)
    return pl.pallas_call(
        functools.partial(dense_kernel, toks, count),
        out_shape=(jax.ShapeDtypeStruct((toks, width), BF16),) * count,
        in_specs=[whole] * (count + 3),
        out_specs=(whole,) * count,
        scratch_shapes=[
            pltpu.VMEM((count * toks, width), BF16),
            pltpu.VMEM((count * toks, width), BF16),
        ],
        compiler_params=pltpu.CompilerParams(vmem_limit_bytes=28 << 20),
        cost_estimate=pl.CostEstimate(
            flops=4 * count * toks * width, bytes_accessed=count * toks, transcendentals=0
        ),
    )(gates, *blocks, up_t, down)


def swap_axis(array, axis):
    count = lax.axis_size(axis)
    return lax.ppermute(array, axis, [(i, i ^ 1) for i in range(count)])


def along_pairs(array, by):
    half = lax.axis_size("ctx") // 2
    pairs = [
        (2 * i + r, (i + by) % half * 2 + r) for i in range(half) for r in range(2)
    ]
    return lax.ppermute(array, "ctx", pairs)


def barrier(*values):
    return lax.optimization_barrier(values)


def add(*parts):
    return sum(part.astype(F32) for part in parts)


def token_experts(expert_in, gates, up_weight, down_weight):
    half = lax.axis_size("ctx") // 2
    up_t = jnp.swapaxes(up_weight, 1, 2)
    turns = [0] + [s for s in (2, 1, 3) if 0 < s < half]
    turns = list(dict.fromkeys(turns))
    come = {0: expert_in}
    for s in turns[1:]:
        come[s] = along_pairs(expert_in, s)
    total = None
    held, block = None, None
    for s in turns:
        same = come[s]
        across = swap_axis(same, "ctx")
        blocks = [same, across, swap_axis(same, "exp"), swap_axis(across, "exp")]
        if held is not None:
            *blocks, _ = barrier(*blocks, held)
        near, far, near_out, far_out = dense_expert(blocks, gates[s], up_t, down_weight)
        far = add(far, swap_axis(far_out, "exp")).astype(BF16)
        held = far
        block = add(near, swap_axis(near_out, "exp"), swap_axis(far, "ctx")).astype(BF16)
        if s:
            block = along_pairs(block, -s)
        total = add(block) if total is None else add(total, block)
    return total


def per_device(
    x_in,
    bc_in,
    z_in,
    time_step,
    decay_log,
    conv_inner,
    conv_bc,
    skip_gain,
    start_state,
    norm_gain,
    out_proj,
    residual,
    moe_gain,
    routes,
    gate_weight,
    up_weight,
    down_weight,
):
    ctx_count = lax.axis_size("ctx")
    exp_count = lax.axis_size("exp")
    exp_index = lax.axis_index("exp")
    block_len = x_in.shape[0]
    local_heads = time_step.shape[1]
    local_groups = bc_in.shape[2] // STATE
    per_group = local_heads // local_groups
    rim_rows = KERNEL - 1
    proj = lax.all_gather(out_proj.T, "ctx", axis=0, tiled=True)

    tok_rows = routes.shape[0]
    top_count = routes.shape[1]
    experts = ctx_count * exp_count * up_weight.shape[0]
    capacity = max(2, 4 * tok_rows * top_count // (3 * experts))
    chosen = routes[:, :, None] == jnp.arange(experts, dtype=jnp.int32)[None, None, :]
    dense_gate = jnp.sum(jnp.where(chosen, gate_weight[:, :, None], 0.0), axis=1)
    log_steps = decay_log.reshape(block_len, local_groups, per_group)
    cumulative = jnp.cumsum(log_steps, axis=0)
    block_log = cumulative[block_len - 1]
    table = jnp.concatenate(
        [dense_gate.T, jnp.pad(block_log.reshape(1, -1), ((0, 0), (0, tok_rows - local_heads)))], 0
    )
    tables = lax.all_gather(table, ("ctx", "exp"), axis=0)
    ctx_index = lax.axis_index("ctx")
    me = ctx_index * exp_count + exp_index
    gates = lax.dynamic_index_in_dim(tables, me, 1, False)
    logs = lax.dynamic_index_in_dim(
        tables[:, experts, :local_heads].reshape(ctx_count, exp_count, local_groups, per_group),
        exp_index,
        1,
        False,
    )
    member = gates > 0.0
    slots = jnp.where(member, jnp.cumsum(member.astype(jnp.int32), axis=1) - 1, -1)

    prev_inner, prev_bc = from_behind(
        (x_in[block_len - rim_rows :], bc_in[block_len - rim_rows :]), "ctx", 1
    )
    inner_act = causal_conv(x_in, prev_inner, conv_inner)
    bc_act = causal_conv(bc_in, prev_bc, conv_bc)
    values = inner_act.astype(F32).reshape(block_len, local_groups, per_group, HEAD_DIM)
    b_rows = bc_act[:, 0].astype(F32).reshape(block_len, local_groups, STATE)
    c_rows = bc_act[:, 1].astype(F32).reshape(block_len, local_groups, STATE)
    step_sizes = time_step.reshape(block_len, local_groups, per_group)
    to_end = jnp.exp(block_log[None] - cumulative) * step_sizes
    end_state = jnp.einsum("tgrp,tgn->grpn", to_end[..., None] * values, b_rows, precision=HIGH)
    entering = entering_state(
        block_log,
        logs,
        end_state,
        start_state.astype(F32).reshape(local_groups, per_group, HEAD_DIM, STATE),
    )
    carried = jnp.exp(cumulative)[..., None] * jnp.einsum(
        "tgn,grpn->tgrp", c_rows, entering, precision=HIGH
    )
    scores = jnp.einsum("tgn,sgn->tsg", c_rows, b_rows, precision=HIGH)
    position = jnp.arange(block_len)
    causal = (position[:, None] >= position[None, :])[:, :, None, None]
    spread_log = cumulative[:, None] - cumulative[None, :]
    decay_table = jnp.where(causal, jnp.exp(jnp.where(causal, spread_log, 0.0)), 0.0)
    mix_table = decay_table * step_sizes[None] * scores[..., None]
    local_part = jnp.einsum("tsgr,sgrp->tgrp", mix_table, values, precision=HIGH)
    outputs = (
        carried + local_part + skip_gain.reshape(local_groups, per_group)[None, :, :, None] * values
    )
    gated = outputs.reshape(block_len, local_groups, -1) * jax.nn.silu(
        z_in.astype(F32).reshape(block_len, local_groups, -1)
    )
    mean_square = jnp.mean(gated * gated, axis=-1, keepdims=True)
    normed = (
        (gated * lax.rsqrt(mean_square + EPS) * norm_gain.astype(F32).reshape(local_groups, -1))
        .reshape(block_len, -1)
        .astype(BF16)
    )

    def projected(part):
        rows = lax.dynamic_slice_in_dim(normed, part * tok_rows, tok_rows, 0)
        return lax.dot_general(rows, proj, (((1,), (1,)), ((), ())), preferred_element_type=F32)

    theirs = lax.ppermute(projected(1 - exp_index), "exp", [(0, 1), (1, 0)])
    mixed = projected(exp_index) + theirs
    hidden_f = (residual.astype(F32) + mixed).astype(BF16).astype(F32)
    expert_in = (
        hidden_f
        * lax.rsqrt(jnp.mean(hidden_f * hidden_f, axis=-1, keepdims=True) + EPS)
        * moe_gain.astype(F32)
    ).astype(BF16)
    half = ctx_count // 2
    if ctx_count % 2 == 0 and 1 < half <= 4 and exp_count == 2:
        shift, place = jnp.arange(half)[:, None], jnp.arange(4)[None, :]
        source = (
            (ctx_index // 2 - shift) % half * 4
            + (ctx_index + place) % 2 * 2
            + (exp_index + place // 2) % 2
        )
        combined = token_experts(
            expert_in, gates[source].reshape(half, -1, 1), up_weight, down_weight
        )
    else:
        tokens = lax.all_gather(expert_in, ("ctx", "exp"), axis=0, tiled=True)
        answers = run_expert(tokens, slots, gates, up_weight, down_weight, capacity)
        combined = lax.psum_scatter(answers, ("ctx", "exp"), scatter_dimension=0, tiled=True)
    return (hidden_f + combined.astype(F32)).astype(BF16)


def solution(mesh):
    in_specs = (
        P(("groups", "ctx"), "exp"),
        P(("groups", "ctx"), None, "exp"),
        P(("groups", "ctx"), "exp"),
        P(("groups", "ctx"), "exp"),
        P(("groups", "ctx"), "exp"),
        P(None, "exp"),
        P(None, None, "exp"),
        P("exp"),
        P(("groups", "exp"), None, None),
        P("exp"),
        P("exp", "ctx"),
        P(("groups", "ctx", "exp"), None),
        P(),
        P(("groups", "ctx", "exp"), None),
        P(("groups", "ctx", "exp"), None),
        P(("ctx", "exp"), None, None),
        P(("ctx", "exp"), None, None),
    )
    out_specs = P(("groups", "ctx", "exp"), None)
    return jax.shard_map(
        per_device, mesh=mesh, in_specs=in_specs, out_specs=out_specs, check_vma=False
    )
```

```python
import functools

import jax
import jax.numpy as jnp
from jax import lax
from jax.experimental import pallas as pl
from jax.experimental.pallas import tpu as pltpu
from jax.sharding import PartitionSpec as P

HEAD_DIM = 64
STATE = 128
KERNEL = 4


EPS = 1e-05
HIGH = lax.Precision.HIGHEST
BF16 = jnp.bfloat16
F32 = jnp.float32


def from_behind(array, axis, by):
    count = lax.axis_size(axis)
    pairs = [(i, i + by) for i in range(count) if 0 <= i + by < count]
    return lax.ppermute(array, axis, pairs)


def entering_state(block_log, logs, end_state, start_state):
    count, index = lax.axis_size("ctx"), lax.axis_index("ctx")
    earlier = (jnp.arange(count) < index).astype(F32)[:, None, None]
    masked = logs * earlier
    after = jnp.flip(jnp.cumsum(jnp.flip(masked, 0), axis=0), 0) - masked
    whole = jnp.sum(masked, axis=0)

    def spread(coefficient):
        return jnp.exp(coefficient)[..., None, None]

    partner = lax.ppermute(
        end_state.astype(BF16), "ctx", [(i, i ^ 1) for i in range(count)]
    ).astype(F32)
    odd = index % 2
    first_log = jnp.where(odd == 1, block_log, lax.dynamic_index_in_dim(logs, index ^ 1, 0, False))
    pair = jnp.where(
        odd == 1,
        spread(first_log) * partner + end_state,
        spread(first_log) * end_state + partner,
    ).astype(BF16)
    entering = spread(whole) * start_state + jnp.where(odd == 1, partner, 0.0)
    half = count // 2

    def after_pair(back):
        place = jnp.maximum((index // 2 - back) * 2 + 1, 0)
        return lax.dynamic_index_in_dim(after, place, 0, False)

    if half <= 4:
        for back in range(half - 1, 0, -1):
            entering = entering + spread(after_pair(back)) * from_behind(
                pair, "ctx", 2 * back
            ).astype(F32)
        return entering
    window = from_behind(pair, "ctx", 2).astype(F32)
    to_start = jnp.where(odd == 1, lax.dynamic_index_in_dim(logs, index ^ 1, 0, False), 0.0)
    back = 1
    while back < half - 1:
        step_log = after_pair(back + 1) - to_start
        window = window + spread(step_log) * from_behind(
            window.astype(BF16), "ctx", 2 * back
        ).astype(F32)
        back *= 2
    return entering + spread(to_start) * window


def causal_conv(sequence, previous, taps):
    length = sequence.shape[0]
    padded = jnp.concatenate([previous, sequence], 0).astype(F32)
    summed = jnp.zeros(sequence.shape, F32)
    for offset in range(taps.shape[0]):
        summed = summed + taps[offset].astype(F32) * padded[offset : offset + length]
    return jax.nn.silu(summed).astype(BF16)


def expert_kernel(cap, tok_rows, pairs, slot_ref, gate_ref, x_ref, up_ref, down_ref, out_ref, sel_ref, ans_ref):
    rows = 2 * cap
    toks = 2 * tok_rows
    def one_hot(i):
        slots = slot_ref[0, :, i * toks : (i + 1) * toks]
        place = lax.broadcasted_iota(jnp.int32, (rows, toks), 0)
        return (place == slots).astype(F32).astype(BF16)

    for i in range(pairs):
        sel_ref[i * rows : (i + 1) * rows, :] = jnp.dot(
            one_hot(i), x_ref[i * toks : (i + 1) * toks, :], preferred_element_type=F32
        ).astype(BF16)
    inner = jnp.dot(sel_ref[...], up_ref[0], preferred_element_type=F32)
    inner = jnp.square(jnp.maximum(inner, 0.0)).astype(BF16)
    ans_ref[...] = jnp.dot(inner, down_ref[0], preferred_element_type=F32).astype(BF16)
    for i in range(pairs):
        spread = lax.dot_general(
            one_hot(i),
            ans_ref[i * rows : (i + 1) * rows, :],
            (((0,), (0,)), ((), ())),
            preferred_element_type=F32,
        )
        out_ref[i * toks : (i + 1) * toks, :] = (
            spread * gate_ref[i * toks : (i + 1) * toks, :]
        ).astype(BF16)


def run_expert(tokens, slots, gates, up_weight, down_weight, cap):
    sources, tok_rows = slots.shape
    width, hidden = up_weight.shape[1:]
    pairs = 2 if cap >= 64 else 4
    step = 2 * pairs
    offset = (jnp.arange(sources, dtype=jnp.int32) % 2 * cap)[:, None]
    slots = jnp.where(slots >= 0, slots + offset, -1).reshape(sources // step, 1, step * tok_rows)
    total = sources * tok_rows
    block = step * tok_rows
    return pl.pallas_call(
        functools.partial(expert_kernel, cap, tok_rows, pairs),
        out_shape=jax.ShapeDtypeStruct((total, width), BF16),
        grid=(sources // step,),
        in_specs=[
            pl.BlockSpec((1, 1, block), lambda i: (i, 0, 0)),
            pl.BlockSpec((block, 1), lambda i: (i, 0)),
            pl.BlockSpec((block, width), lambda i: (i, 0)),
            pl.BlockSpec((1, width, hidden), lambda i: (0, 0, 0), pipeline_mode=pl.Buffered(1)),
            pl.BlockSpec((1, hidden, width), lambda i: (0, 0, 0), pipeline_mode=pl.Buffered(1)),
        ],
        out_specs=pl.BlockSpec((block, width), lambda i: (i, 0)),
        scratch_shapes=[
            pltpu.VMEM((step * cap, width), BF16),
            pltpu.VMEM((step * cap, width), BF16),
        ],
        compiler_params=pltpu.CompilerParams(
            dimension_semantics=("arbitrary",), vmem_limit_bytes=56 << 20
        ),
        cost_estimate=pl.CostEstimate(
            flops=4 * sources * cap * width * hidden,
            bytes_accessed=4 * total * width + 4 * width * hidden,
            transcendentals=0,
        ),
    )(slots, gates.reshape(total, 1), tokens, up_weight, down_weight)


def dot_t(a, b):
    return lax.dot_general(a, b, (((1,), (1,)), ((), ())), preferred_element_type=F32)


def dense_kernel(toks, count, gate_ref, *refs):
    blocks = refs[:count]
    up_ref, down_ref = refs[count : count + 2]
    outs = refs[count + 2 : 2 * count + 2]
    x_ref, y_ref = refs[2 * count + 2 :]
    for j in range(count):
        x_ref[j * toks : (j + 1) * toks, :] = blocks[j][...]
    size = 2 * toks

    def part(n, carry):
        rows = pl.ds(pl.multiple_of(n * size, size), size)
        inner = dot_t(x_ref[rows, :], up_ref[0])
        inner = jnp.square(jnp.maximum(inner, 0.0)).astype(BF16)
        answers = jnp.dot(inner, down_ref[0], preferred_element_type=F32)
        y_ref[rows, :] = (answers.astype(BF16).astype(F32) * gate_ref[rows, :]).astype(BF16)
        return carry

    lax.fori_loop(0, count // 2, part, 0)
    for j in range(count):
        outs[j][...] = y_ref[j * toks : (j + 1) * toks, :]


def dense_expert(blocks, gates, up_t, down):
    toks, width = blocks[0].shape
    hidden = up_t.shape[1]
    count = len(blocks)
    whole = pl.BlockSpec(memory_space=pltpu.VMEM)
    return pl.pallas_call(
        functools.partial(dense_kernel, toks, count),
        out_shape=(jax.ShapeDtypeStruct((toks, width), BF16),) * count,
        in_specs=[whole] * (count + 3),
        out_specs=(whole,) * count,
        scratch_shapes=[
            pltpu.VMEM((count * toks, width), BF16),
            pltpu.VMEM((count * toks, width), BF16),
        ],
        compiler_params=pltpu.CompilerParams(vmem_limit_bytes=28 << 20),
        cost_estimate=pl.CostEstimate(
            flops=4 * count * toks * width, bytes_accessed=count * toks, transcendentals=0
        ),
    )(gates, *blocks, up_t, down)


def swap_axis(array, axis):
    count = lax.axis_size(axis)
    return lax.ppermute(array, axis, [(i, i ^ 1) for i in range(count)])


def along_pairs(array, by):
    half = lax.axis_size("ctx") // 2
    pairs = [
        (2 * i + r, (i + by) % half * 2 + r) for i in range(half) for r in range(2)
    ]
    return lax.ppermute(array, "ctx", pairs)


def barrier(*values):
    return lax.optimization_barrier(values)


def add(*parts):
    return sum(part.astype(F32) for part in parts)


def token_experts(expert_in, gates, up_weight, down_weight):
    half = lax.axis_size("ctx") // 2
    up_t = jnp.swapaxes(up_weight, 1, 2)
    turns = [0] + [s for s in (1, 3, 2) if 0 < s < half]
    turns = list(dict.fromkeys(turns))
    come = {0: expert_in}
    for s in turns[1:]:
        come[s] = along_pairs(expert_in, s)
    total = None
    held, block = None, None
    for s in turns:
        same = come[s]
        across = swap_axis(same, "ctx")
        blocks = [same, across, swap_axis(same, "exp"), swap_axis(across, "exp")]
        if held is not None:
            *blocks, _ = barrier(*blocks, held)
        near, far, near_out, far_out = dense_expert(blocks, gates[s], up_t, down_weight)
        far = add(far, swap_axis(far_out, "exp")).astype(BF16)
        held = far
        near = add(near, swap_axis(near_out, "exp"))
        if s == 0:
            home = near.astype(BF16), far
            continue
        block = add(near, swap_axis(far, "ctx")).astype(BF16)
        last = block
        block = along_pairs(block, -s)
        total = add(block) if total is None else add(total, block)
    near, far, _ = barrier(*home, last)
    return add(total, near, swap_axis(far, "ctx"))


def per_device(
    x_in,
    bc_in,
    z_in,
    time_step,
    decay_log,
    conv_inner,
    conv_bc,
    skip_gain,
    start_state,
    norm_gain,
    out_proj,
    residual,
    moe_gain,
    routes,
    gate_weight,
    up_weight,
    down_weight,
):
    ctx_count = lax.axis_size("ctx")
    exp_count = lax.axis_size("exp")
    exp_index = lax.axis_index("exp")
    block_len = x_in.shape[0]
    local_heads = time_step.shape[1]
    local_groups = bc_in.shape[2] // STATE
    per_group = local_heads // local_groups
    rim_rows = KERNEL - 1
    proj = lax.all_gather(out_proj.T, "ctx", axis=0, tiled=True)

    tok_rows = routes.shape[0]
    top_count = routes.shape[1]
    experts = ctx_count * exp_count * up_weight.shape[0]
    capacity = max(2, 4 * tok_rows * top_count // (3 * experts))
    chosen = routes[:, :, None] == jnp.arange(experts, dtype=jnp.int32)[None, None, :]
    dense_gate = jnp.sum(jnp.where(chosen, gate_weight[:, :, None], 0.0), axis=1)
    log_steps = decay_log.reshape(block_len, local_groups, per_group)
    cumulative = jnp.cumsum(log_steps, axis=0)
    block_log = cumulative[block_len - 1]
    table = jnp.concatenate(
        [dense_gate.T, jnp.pad(block_log.reshape(1, -1), ((0, 0), (0, tok_rows - local_heads)))], 0
    )
    tables = lax.all_gather(table, ("ctx", "exp"), axis=0)
    ctx_index = lax.axis_index("ctx")
    me = ctx_index * exp_count + exp_index
    gates = lax.dynamic_index_in_dim(tables, me, 1, False)
    logs = lax.dynamic_index_in_dim(
        tables[:, experts, :local_heads].reshape(ctx_count, exp_count, local_groups, per_group),
        exp_index,
        1,
        False,
    )
    member = gates > 0.0
    slots = jnp.where(member, jnp.cumsum(member.astype(jnp.int32), axis=1) - 1, -1)

    prev_inner, prev_bc = from_behind(
        (x_in[block_len - rim_rows :], bc_in[block_len - rim_rows :]), "ctx", 1
    )
    inner_act = causal_conv(x_in, prev_inner, conv_inner)
    bc_act = causal_conv(bc_in, prev_bc, conv_bc)
    values = inner_act.astype(F32).reshape(block_len, local_groups, per_group, HEAD_DIM)
    b_rows = bc_act[:, 0].astype(F32).reshape(block_len, local_groups, STATE)
    c_rows = bc_act[:, 1].astype(F32).reshape(block_len, local_groups, STATE)
    step_sizes = time_step.reshape(block_len, local_groups, per_group)
    to_end = jnp.exp(block_log[None] - cumulative) * step_sizes
    end_state = jnp.einsum("tgrp,tgn->grpn", to_end[..., None] * values, b_rows, precision=HIGH)
    entering = entering_state(
        block_log,
        logs,
        end_state,
        start_state.astype(F32).reshape(local_groups, per_group, HEAD_DIM, STATE),
    )
    carried = jnp.exp(cumulative)[..., None] * jnp.einsum(
        "tgn,grpn->tgrp", c_rows, entering, precision=HIGH
    )
    scores = jnp.einsum("tgn,sgn->tsg", c_rows, b_rows, precision=HIGH)
    position = jnp.arange(block_len)
    causal = (position[:, None] >= position[None, :])[:, :, None, None]
    spread_log = cumulative[:, None] - cumulative[None, :]
    decay_table = jnp.where(causal, jnp.exp(jnp.where(causal, spread_log, 0.0)), 0.0)
    mix_table = decay_table * step_sizes[None] * scores[..., None]
    local_part = jnp.einsum("tsgr,sgrp->tgrp", mix_table, values, precision=HIGH)
    outputs = (
        carried + local_part + skip_gain.reshape(local_groups, per_group)[None, :, :, None] * values
    )
    gated = outputs.reshape(block_len, local_groups, -1) * jax.nn.silu(
        z_in.astype(F32).reshape(block_len, local_groups, -1)
    )
    mean_square = jnp.mean(gated * gated, axis=-1, keepdims=True)
    normed = (
        (gated * lax.rsqrt(mean_square + EPS) * norm_gain.astype(F32).reshape(local_groups, -1))
        .reshape(block_len, -1)
        .astype(BF16)
    )

    def projected(part):
        rows = lax.dynamic_slice_in_dim(normed, part * tok_rows, tok_rows, 0)
        return lax.dot_general(rows, proj, (((1,), (1,)), ((), ())), preferred_element_type=F32)

    theirs = lax.ppermute(projected(1 - exp_index), "exp", [(0, 1), (1, 0)])
    mixed = projected(exp_index) + theirs
    hidden_f = (residual.astype(F32) + mixed).astype(BF16).astype(F32)
    expert_in = (
        hidden_f
        * lax.rsqrt(jnp.mean(hidden_f * hidden_f, axis=-1, keepdims=True) + EPS)
        * moe_gain.astype(F32)
    ).astype(BF16)
    half = ctx_count // 2
    if ctx_count % 2 == 0 and 1 < half <= 4 and exp_count == 2:
        shift, place = jnp.arange(half)[:, None], jnp.arange(4)[None, :]
        source = (
            (ctx_index // 2 - shift) % half * 4
            + (ctx_index + place) % 2 * 2
            + (exp_index + place // 2) % 2
        )
        combined = token_experts(
            expert_in, gates[source].reshape(half, -1, 1), up_weight, down_weight
        )
    else:
        tokens = lax.all_gather(expert_in, ("ctx", "exp"), axis=0, tiled=True)
        answers = run_expert(tokens, slots, gates, up_weight, down_weight, capacity)
        combined = lax.psum_scatter(answers, ("ctx", "exp"), scatter_dimension=0, tiled=True)
    return (hidden_f + combined.astype(F32)).astype(BF16)


def solution(mesh):
    in_specs = (
        P(("groups", "ctx"), "exp"),
        P(("groups", "ctx"), None, "exp"),
        P(("groups", "ctx"), "exp"),
        P(("groups", "ctx"), "exp"),
        P(("groups", "ctx"), "exp"),
        P(None, "exp"),
        P(None, None, "exp"),
        P("exp"),
        P(("groups", "exp"), None, None),
        P("exp"),
        P("exp", "ctx"),
        P(("groups", "ctx", "exp"), None),
        P(),
        P(("groups", "ctx", "exp"), None),
        P(("groups", "ctx", "exp"), None),
        P(("ctx", "exp"), None, None),
        P(("ctx", "exp"), None, None),
    )
    out_specs = P(("groups", "ctx", "exp"), None)
    return jax.shard_map(
        per_device, mesh=mesh, in_specs=in_specs, out_specs=out_specs, check_vma=False
    )
```

```python
import functools

import jax
import jax.numpy as jnp
from jax import lax
from jax.experimental import pallas as pl
from jax.experimental.pallas import tpu as pltpu
from jax.sharding import PartitionSpec as P

HEAD_DIM = 64
STATE = 128
KERNEL = 4


EPS = 1e-05
HIGH = lax.Precision.HIGHEST
BF16 = jnp.bfloat16
F32 = jnp.float32


def from_behind(array, axis, by):
    count = lax.axis_size(axis)
    pairs = [(i, i + by) for i in range(count) if 0 <= i + by < count]
    return lax.ppermute(array, axis, pairs)


def entering_state(block_log, logs, end_state, start_state):
    count, index = lax.axis_size("ctx"), lax.axis_index("ctx")
    earlier = (jnp.arange(count) < index).astype(F32)[:, None, None]
    masked = logs * earlier
    after = jnp.flip(jnp.cumsum(jnp.flip(masked, 0), axis=0), 0) - masked
    whole = jnp.sum(masked, axis=0)

    def spread(coefficient):
        return jnp.exp(coefficient)[..., None, None]

    partner = lax.ppermute(
        end_state.astype(BF16), "ctx", [(i, i ^ 1) for i in range(count)]
    ).astype(F32)
    odd = index % 2
    first_log = jnp.where(odd == 1, block_log, lax.dynamic_index_in_dim(logs, index ^ 1, 0, False))
    pair = jnp.where(
        odd == 1,
        spread(first_log) * partner + end_state,
        spread(first_log) * end_state + partner,
    ).astype(BF16)
    entering = spread(whole) * start_state + jnp.where(odd == 1, partner, 0.0)
    half = count // 2

    def after_pair(back):
        place = jnp.maximum((index // 2 - back) * 2 + 1, 0)
        return lax.dynamic_index_in_dim(after, place, 0, False)

    if half <= 4:
        for back in range(half - 1, 0, -1):
            entering = entering + spread(after_pair(back)) * from_behind(
                pair, "ctx", 2 * back
            ).astype(F32)
        return entering
    window = from_behind(pair, "ctx", 2).astype(F32)
    to_start = jnp.where(odd == 1, lax.dynamic_index_in_dim(logs, index ^ 1, 0, False), 0.0)
    back = 1
    while back < half - 1:
        step_log = after_pair(back + 1) - to_start
        window = window + spread(step_log) * from_behind(
            window.astype(BF16), "ctx", 2 * back
        ).astype(F32)
        back *= 2
    return entering + spread(to_start) * window


def causal_conv(sequence, previous, taps):
    length = sequence.shape[0]
    padded = jnp.concatenate([previous, sequence], 0).astype(F32)
    summed = jnp.zeros(sequence.shape, F32)
    for offset in range(taps.shape[0]):
        summed = summed + taps[offset].astype(F32) * padded[offset : offset + length]
    return jax.nn.silu(summed).astype(BF16)


def expert_kernel(cap, tok_rows, pairs, slot_ref, gate_ref, x_ref, up_ref, down_ref, out_ref, sel_ref, ans_ref):
    rows = 2 * cap
    toks = 2 * tok_rows
    def one_hot(i):
        slots = slot_ref[0, :, i * toks : (i + 1) * toks]
        place = lax.broadcasted_iota(jnp.int32, (rows, toks), 0)
        return (place == slots).astype(F32).astype(BF16)

    for i in range(pairs):
        sel_ref[i * rows : (i + 1) * rows, :] = jnp.dot(
            one_hot(i), x_ref[i * toks : (i + 1) * toks, :], preferred_element_type=F32
        ).astype(BF16)
    inner = jnp.dot(sel_ref[...], up_ref[0], preferred_element_type=F32)
    inner = jnp.square(jnp.maximum(inner, 0.0)).astype(BF16)
    ans_ref[...] = jnp.dot(inner, down_ref[0], preferred_element_type=F32).astype(BF16)
    for i in range(pairs):
        spread = lax.dot_general(
            one_hot(i),
            ans_ref[i * rows : (i + 1) * rows, :],
            (((0,), (0,)), ((), ())),
            preferred_element_type=F32,
        )
        out_ref[i * toks : (i + 1) * toks, :] = (
            spread * gate_ref[i * toks : (i + 1) * toks, :]
        ).astype(BF16)


def run_expert(tokens, slots, gates, up_weight, down_weight, cap):
    sources, tok_rows = slots.shape
    width, hidden = up_weight.shape[1:]
    pairs = 2 if cap >= 64 else 4
    step = 2 * pairs
    offset = (jnp.arange(sources, dtype=jnp.int32) % 2 * cap)[:, None]
    slots = jnp.where(slots >= 0, slots + offset, -1).reshape(sources // step, 1, step * tok_rows)
    total = sources * tok_rows
    block = step * tok_rows
    return pl.pallas_call(
        functools.partial(expert_kernel, cap, tok_rows, pairs),
        out_shape=jax.ShapeDtypeStruct((total, width), BF16),
        grid=(sources // step,),
        in_specs=[
            pl.BlockSpec((1, 1, block), lambda i: (i, 0, 0)),
            pl.BlockSpec((block, 1), lambda i: (i, 0)),
            pl.BlockSpec((block, width), lambda i: (i, 0)),
            pl.BlockSpec((1, width, hidden), lambda i: (0, 0, 0), pipeline_mode=pl.Buffered(1)),
            pl.BlockSpec((1, hidden, width), lambda i: (0, 0, 0), pipeline_mode=pl.Buffered(1)),
        ],
        out_specs=pl.BlockSpec((block, width), lambda i: (i, 0)),
        scratch_shapes=[
            pltpu.VMEM((step * cap, width), BF16),
            pltpu.VMEM((step * cap, width), BF16),
        ],
        compiler_params=pltpu.CompilerParams(
            dimension_semantics=("arbitrary",), vmem_limit_bytes=56 << 20
        ),
        cost_estimate=pl.CostEstimate(
            flops=4 * sources * cap * width * hidden,
            bytes_accessed=4 * total * width + 4 * width * hidden,
            transcendentals=0,
        ),
    )(slots, gates.reshape(total, 1), tokens, up_weight, down_weight)


def dot_t(a, b):
    return lax.dot_general(a, b, (((1,), (1,)), ((), ())), preferred_element_type=F32)


def dense_kernel(toks, count, gate_ref, *refs):
    blocks = refs[:count]
    up_hbm, down_hbm = refs[count : count + 2]
    outs = refs[count + 2 : 2 * count + 2]
    x_ref, y_ref, up_ref, down_ref, sems = refs[2 * count + 2 :]
    up_copy = pltpu.make_async_copy(up_hbm, up_ref, sems.at[0])
    down_copy = pltpu.make_async_copy(down_hbm, down_ref, sems.at[1])
    up_copy.start()
    down_copy.start()
    for j in range(count):
        x_ref[j * toks : (j + 1) * toks, :] = blocks[j][...]
    size = 2 * toks
    up_copy.wait()

    def part(n, carry):
        rows = pl.ds(pl.multiple_of(n * size, size), size)
        inner = dot_t(x_ref[rows, :], up_ref[0])
        inner = jnp.square(jnp.maximum(inner, 0.0)).astype(BF16)
        pl.when(n == 0)(down_copy.wait)
        answers = jnp.dot(inner, down_ref[0], preferred_element_type=F32)
        y_ref[rows, :] = (answers.astype(BF16).astype(F32) * gate_ref[rows, :]).astype(BF16)
        return carry

    lax.fori_loop(0, count // 2, part, 0)
    for j in range(count):
        outs[j][...] = y_ref[j * toks : (j + 1) * toks, :]


def dense_expert(blocks, gates, up_t, down):
    toks, width = blocks[0].shape
    hidden = up_t.shape[1]
    count = len(blocks)
    whole = pl.BlockSpec(memory_space=pltpu.VMEM)
    return pl.pallas_call(
        functools.partial(dense_kernel, toks, count),
        out_shape=(jax.ShapeDtypeStruct((toks, width), BF16),) * count,
        in_specs=[whole] * (count + 1) + [pl.BlockSpec(memory_space=pl.ANY)] * 2,
        out_specs=(whole,) * count,
        scratch_shapes=[
            pltpu.VMEM((count * toks, width), BF16),
            pltpu.VMEM((count * toks, width), BF16),
            pltpu.VMEM((1, hidden, width), BF16),
            pltpu.VMEM((1, hidden, width), BF16),
            pltpu.SemaphoreType.DMA((2,)),
        ],
        compiler_params=pltpu.CompilerParams(vmem_limit_bytes=40 << 20),
        cost_estimate=pl.CostEstimate(
            flops=4 * count * toks * width, bytes_accessed=count * toks, transcendentals=0
        ),
    )(gates, *blocks, up_t, down)


def swap_axis(array, axis):
    count = lax.axis_size(axis)
    return lax.ppermute(array, axis, [(i, i ^ 1) for i in range(count)])


def along_pairs(array, by):
    half = lax.axis_size("ctx") // 2
    pairs = [
        (2 * i + r, (i + by) % half * 2 + r) for i in range(half) for r in range(2)
    ]
    return lax.ppermute(array, "ctx", pairs)


def barrier(*values):
    return lax.optimization_barrier(values)


def add(*parts):
    return sum(part.astype(F32) for part in parts)


def token_experts(expert_in, gates, up_weight, down_weight):
    half = lax.axis_size("ctx") // 2
    up_t = jnp.swapaxes(up_weight, 1, 2)
    turns = [0] + [s for s in (1, 3, 2) if 0 < s < half]
    turns = list(dict.fromkeys(turns))
    come = {0: expert_in}
    for s in turns[1:]:
        come[s] = along_pairs(expert_in, s)
    total = None
    held, block = None, None
    for s in turns:
        same = come[s]
        across = swap_axis(same, "ctx")
        blocks = [same, across, swap_axis(same, "exp"), swap_axis(across, "exp")]
        if held is not None:
            *blocks, _ = barrier(*blocks, held)
        near, far, near_out, far_out = dense_expert(blocks, gates[s], up_t, down_weight)
        far = add(far, swap_axis(far_out, "exp")).astype(BF16)
        held = far
        near = add(near, swap_axis(near_out, "exp"))
        if s == 0:
            home = near.astype(BF16), far
            continue
        block = add(near, swap_axis(far, "ctx")).astype(BF16)
        last = block
        block = along_pairs(block, -s)
        total = add(block) if total is None else add(total, block)
    near, far, _ = barrier(*home, last)
    return add(total, near, swap_axis(far, "ctx"))


def per_device(
    x_in,
    bc_in,
    z_in,
    time_step,
    decay_log,
    conv_inner,
    conv_bc,
    skip_gain,
    start_state,
    norm_gain,
    out_proj,
    residual,
    moe_gain,
    routes,
    gate_weight,
    up_weight,
    down_weight,
):
    ctx_count = lax.axis_size("ctx")
    exp_count = lax.axis_size("exp")
    exp_index = lax.axis_index("exp")
    block_len = x_in.shape[0]
    local_heads = time_step.shape[1]
    local_groups = bc_in.shape[2] // STATE
    per_group = local_heads // local_groups
    rim_rows = KERNEL - 1
    proj = lax.all_gather(out_proj.T, "ctx", axis=0, tiled=True)

    tok_rows = routes.shape[0]
    top_count = routes.shape[1]
    experts = ctx_count * exp_count * up_weight.shape[0]
    capacity = max(2, 4 * tok_rows * top_count // (3 * experts))
    chosen = routes[:, :, None] == jnp.arange(experts, dtype=jnp.int32)[None, None, :]
    dense_gate = jnp.sum(jnp.where(chosen, gate_weight[:, :, None], 0.0), axis=1)
    log_steps = decay_log.reshape(block_len, local_groups, per_group)
    cumulative = jnp.cumsum(log_steps, axis=0)
    block_log = cumulative[block_len - 1]
    table = jnp.concatenate(
        [dense_gate.T, jnp.pad(block_log.reshape(1, -1), ((0, 0), (0, tok_rows - local_heads)))], 0
    )
    tables = lax.all_gather(table, ("ctx", "exp"), axis=0)
    ctx_index = lax.axis_index("ctx")
    me = ctx_index * exp_count + exp_index
    gates = lax.dynamic_index_in_dim(tables, me, 1, False)
    logs = lax.dynamic_index_in_dim(
        tables[:, experts, :local_heads].reshape(ctx_count, exp_count, local_groups, per_group),
        exp_index,
        1,
        False,
    )
    member = gates > 0.0
    slots = jnp.where(member, jnp.cumsum(member.astype(jnp.int32), axis=1) - 1, -1)

    prev_inner, prev_bc = from_behind(
        (x_in[block_len - rim_rows :], bc_in[block_len - rim_rows :]), "ctx", 1
    )
    inner_act = causal_conv(x_in, prev_inner, conv_inner)
    bc_act = causal_conv(bc_in, prev_bc, conv_bc)
    values = inner_act.astype(F32).reshape(block_len, local_groups, per_group, HEAD_DIM)
    b_rows = bc_act[:, 0].astype(F32).reshape(block_len, local_groups, STATE)
    c_rows = bc_act[:, 1].astype(F32).reshape(block_len, local_groups, STATE)
    step_sizes = time_step.reshape(block_len, local_groups, per_group)
    to_end = jnp.exp(block_log[None] - cumulative) * step_sizes
    end_state = jnp.einsum("tgrp,tgn->grpn", to_end[..., None] * values, b_rows, precision=HIGH)
    entering = entering_state(
        block_log,
        logs,
        end_state,
        start_state.astype(F32).reshape(local_groups, per_group, HEAD_DIM, STATE),
    )
    carried = jnp.exp(cumulative)[..., None] * jnp.einsum(
        "tgn,grpn->tgrp", c_rows, entering, precision=HIGH
    )
    scores = jnp.einsum("tgn,sgn->tsg", c_rows, b_rows, precision=HIGH)
    position = jnp.arange(block_len)
    causal = (position[:, None] >= position[None, :])[:, :, None, None]
    spread_log = cumulative[:, None] - cumulative[None, :]
    decay_table = jnp.where(causal, jnp.exp(jnp.where(causal, spread_log, 0.0)), 0.0)
    mix_table = decay_table * step_sizes[None] * scores[..., None]
    local_part = jnp.einsum("tsgr,sgrp->tgrp", mix_table, values, precision=HIGH)
    outputs = (
        carried + local_part + skip_gain.reshape(local_groups, per_group)[None, :, :, None] * values
    )
    gated = outputs.reshape(block_len, local_groups, -1) * jax.nn.silu(
        z_in.astype(F32).reshape(block_len, local_groups, -1)
    )
    mean_square = jnp.mean(gated * gated, axis=-1, keepdims=True)
    normed = (
        (gated * lax.rsqrt(mean_square + EPS) * norm_gain.astype(F32).reshape(local_groups, -1))
        .reshape(block_len, -1)
        .astype(BF16)
    )

    def projected(part):
        rows = lax.dynamic_slice_in_dim(normed, part * tok_rows, tok_rows, 0)
        return lax.dot_general(rows, proj, (((1,), (1,)), ((), ())), preferred_element_type=F32)

    theirs = lax.ppermute(projected(1 - exp_index), "exp", [(0, 1), (1, 0)])
    mixed = projected(exp_index) + theirs
    hidden_f = (residual.astype(F32) + mixed).astype(BF16).astype(F32)
    expert_in = (
        hidden_f
        * lax.rsqrt(jnp.mean(hidden_f * hidden_f, axis=-1, keepdims=True) + EPS)
        * moe_gain.astype(F32)
    ).astype(BF16)
    half = ctx_count // 2
    if ctx_count % 2 == 0 and 1 < half <= 4 and exp_count == 2:
        shift, place = jnp.arange(half)[:, None], jnp.arange(4)[None, :]
        source = (
            (ctx_index // 2 - shift) % half * 4
            + (ctx_index + place) % 2 * 2
            + (exp_index + place // 2) % 2
        )
        combined = token_experts(
            expert_in, gates[source].reshape(half, -1, 1), up_weight, down_weight
        )
    else:
        tokens = lax.all_gather(expert_in, ("ctx", "exp"), axis=0, tiled=True)
        answers = run_expert(tokens, slots, gates, up_weight, down_weight, capacity)
        combined = lax.psum_scatter(answers, ("ctx", "exp"), scatter_dimension=0, tiled=True)
    return (hidden_f + combined.astype(F32)).astype(BF16)


def solution(mesh):
    in_specs = (
        P(("groups", "ctx"), "exp"),
        P(("groups", "ctx"), None, "exp"),
        P(("groups", "ctx"), "exp"),
        P(("groups", "ctx"), "exp"),
        P(("groups", "ctx"), "exp"),
        P(None, "exp"),
        P(None, None, "exp"),
        P("exp"),
        P(("groups", "exp"), None, None),
        P("exp"),
        P("exp", "ctx"),
        P(("groups", "ctx", "exp"), None),
        P(),
        P(("groups", "ctx", "exp"), None),
        P(("groups", "ctx", "exp"), None),
        P(("ctx", "exp"), None, None),
        P(("ctx", "exp"), None, None),
    )
    out_specs = P(("groups", "ctx", "exp"), None)
    return jax.shard_map(
        per_device, mesh=mesh, in_specs=in_specs, out_specs=out_specs, check_vma=False
    )
```

```python
import functools

import jax
import jax.numpy as jnp
from jax import lax
from jax.experimental import pallas as pl
from jax.experimental.pallas import tpu as pltpu
from jax.sharding import PartitionSpec as P

HEAD_DIM = 64
STATE = 128
KERNEL = 4


EPS = 1e-05
HIGH = lax.Precision.HIGHEST
BF16 = jnp.bfloat16
F32 = jnp.float32


def from_behind(array, axis, by):
    count = lax.axis_size(axis)
    pairs = [(i, i + by) for i in range(count) if 0 <= i + by < count]
    return lax.ppermute(array, axis, pairs)


def entering_state(block_log, logs, end_state, start_state):
    count, index = lax.axis_size("ctx"), lax.axis_index("ctx")
    earlier = (jnp.arange(count) < index).astype(F32)[:, None, None]
    masked = logs * earlier
    after = jnp.flip(jnp.cumsum(jnp.flip(masked, 0), axis=0), 0) - masked
    whole = jnp.sum(masked, axis=0)

    def spread(coefficient):
        return jnp.exp(coefficient)[..., None, None]

    partner = lax.ppermute(
        end_state.astype(BF16), "ctx", [(i, i ^ 1) for i in range(count)]
    ).astype(F32)
    odd = index % 2
    first_log = jnp.where(odd == 1, block_log, lax.dynamic_index_in_dim(logs, index ^ 1, 0, False))
    pair = jnp.where(
        odd == 1,
        spread(first_log) * partner + end_state,
        spread(first_log) * end_state + partner,
    ).astype(BF16)
    entering = spread(whole) * start_state + jnp.where(odd == 1, partner, 0.0)
    half = count // 2

    def after_pair(back):
        place = jnp.maximum((index // 2 - back) * 2 + 1, 0)
        return lax.dynamic_index_in_dim(after, place, 0, False)

    if half <= 4:
        for back in range(half - 1, 0, -1):
            entering = entering + spread(after_pair(back)) * from_behind(
                pair, "ctx", 2 * back
            ).astype(F32)
        return entering
    window = from_behind(pair, "ctx", 2).astype(F32)
    to_start = jnp.where(odd == 1, lax.dynamic_index_in_dim(logs, index ^ 1, 0, False), 0.0)
    back = 1
    while back < half - 1:
        step_log = after_pair(back + 1) - to_start
        window = window + spread(step_log) * from_behind(
            window.astype(BF16), "ctx", 2 * back
        ).astype(F32)
        back *= 2
    return entering + spread(to_start) * window


def causal_conv(sequence, previous, taps):
    length = sequence.shape[0]
    padded = jnp.concatenate([previous, sequence], 0).astype(F32)
    summed = jnp.zeros(sequence.shape, F32)
    for offset in range(taps.shape[0]):
        summed = summed + taps[offset].astype(F32) * padded[offset : offset + length]
    return jax.nn.silu(summed).astype(BF16)


def expert_kernel(cap, tok_rows, pairs, slot_ref, gate_ref, x_ref, up_ref, down_ref, out_ref, sel_ref, ans_ref):
    rows = 2 * cap
    toks = 2 * tok_rows
    def one_hot(i):
        slots = slot_ref[0, :, i * toks : (i + 1) * toks]
        place = lax.broadcasted_iota(jnp.int32, (rows, toks), 0)
        return (place == slots).astype(F32).astype(BF16)

    for i in range(pairs):
        sel_ref[i * rows : (i + 1) * rows, :] = jnp.dot(
            one_hot(i), x_ref[i * toks : (i + 1) * toks, :], preferred_element_type=F32
        ).astype(BF16)
    inner = jnp.dot(sel_ref[...], up_ref[0], preferred_element_type=F32)
    inner = jnp.square(jnp.maximum(inner, 0.0)).astype(BF16)
    ans_ref[...] = jnp.dot(inner, down_ref[0], preferred_element_type=F32).astype(BF16)
    for i in range(pairs):
        spread = lax.dot_general(
            one_hot(i),
            ans_ref[i * rows : (i + 1) * rows, :],
            (((0,), (0,)), ((), ())),
            preferred_element_type=F32,
        )
        out_ref[i * toks : (i + 1) * toks, :] = (
            spread * gate_ref[i * toks : (i + 1) * toks, :]
        ).astype(BF16)


def run_expert(tokens, slots, gates, up_weight, down_weight, cap):
    sources, tok_rows = slots.shape
    width, hidden = up_weight.shape[1:]
    pairs = 2 if cap >= 64 else 4
    step = 2 * pairs
    offset = (jnp.arange(sources, dtype=jnp.int32) % 2 * cap)[:, None]
    slots = jnp.where(slots >= 0, slots + offset, -1).reshape(sources // step, 1, step * tok_rows)
    total = sources * tok_rows
    block = step * tok_rows
    return pl.pallas_call(
        functools.partial(expert_kernel, cap, tok_rows, pairs),
        out_shape=jax.ShapeDtypeStruct((total, width), BF16),
        grid=(sources // step,),
        in_specs=[
            pl.BlockSpec((1, 1, block), lambda i: (i, 0, 0)),
            pl.BlockSpec((block, 1), lambda i: (i, 0)),
            pl.BlockSpec((block, width), lambda i: (i, 0)),
            pl.BlockSpec((1, width, hidden), lambda i: (0, 0, 0), pipeline_mode=pl.Buffered(1)),
            pl.BlockSpec((1, hidden, width), lambda i: (0, 0, 0), pipeline_mode=pl.Buffered(1)),
        ],
        out_specs=pl.BlockSpec((block, width), lambda i: (i, 0)),
        scratch_shapes=[
            pltpu.VMEM((step * cap, width), BF16),
            pltpu.VMEM((step * cap, width), BF16),
        ],
        compiler_params=pltpu.CompilerParams(
            dimension_semantics=("arbitrary",), vmem_limit_bytes=56 << 20
        ),
        cost_estimate=pl.CostEstimate(
            flops=4 * sources * cap * width * hidden,
            bytes_accessed=4 * total * width + 4 * width * hidden,
            transcendentals=0,
        ),
    )(slots, gates.reshape(total, 1), tokens, up_weight, down_weight)


def dot_t(a, b):
    return lax.dot_general(a, b, (((1,), (1,)), ((), ())), preferred_element_type=F32)


def dense_kernel(toks, count, gate_ref, *refs):
    blocks = refs[:count]
    up_hbm, down_hbm = refs[count : count + 2]
    outs = refs[count + 2 : 2 * count + 2]
    x_ref, y_ref, up_ref, down_ref, sems = refs[2 * count + 2 :]
    up_copy = pltpu.make_async_copy(up_hbm, up_ref, sems.at[0])
    down_copy = pltpu.make_async_copy(down_hbm, down_ref, sems.at[1])
    up_copy.start()
    down_copy.start()
    for j in range(count):
        x_ref[j * toks : (j + 1) * toks, :] = blocks[j][...]
    size = 2 * toks
    up_copy.wait()

    def part(n, carry):
        rows = pl.ds(pl.multiple_of(n * size, size), size)
        inner = dot_t(x_ref[rows, :], up_ref[0])
        inner = jnp.square(jnp.maximum(inner, 0.0)).astype(BF16)
        pl.when(n == 0)(down_copy.wait)
        answers = jnp.dot(inner, down_ref[0], preferred_element_type=F32)
        y_ref[rows, :] = (answers.astype(BF16).astype(F32) * gate_ref[rows, :]).astype(BF16)
        return carry

    lax.fori_loop(0, count // 2, part, 0)
    for j in range(count):
        outs[j][...] = y_ref[j * toks : (j + 1) * toks, :]


def dense_expert(blocks, gates, up_t, down):
    toks, width = blocks[0].shape
    hidden = up_t.shape[1]
    count = len(blocks)
    whole = pl.BlockSpec(memory_space=pltpu.VMEM)
    return pl.pallas_call(
        functools.partial(dense_kernel, toks, count),
        out_shape=(jax.ShapeDtypeStruct((toks, width), BF16),) * count,
        in_specs=[whole] * (count + 1) + [pl.BlockSpec(memory_space=pl.ANY)] * 2,
        out_specs=(whole,) * count,
        scratch_shapes=[
            pltpu.VMEM((count * toks, width), BF16),
            pltpu.VMEM((count * toks, width), BF16),
            pltpu.VMEM((1, hidden, width), BF16),
            pltpu.VMEM((1, hidden, width), BF16),
            pltpu.SemaphoreType.DMA((2,)),
        ],
        compiler_params=pltpu.CompilerParams(vmem_limit_bytes=40 << 20),
        cost_estimate=pl.CostEstimate(
            flops=4 * count * toks * width * hidden,
            bytes_accessed=4 * width * (count * toks + hidden),
            transcendentals=0,
        ),
    )(gates, *blocks, up_t, down)


def swap_axis(array, axis):
    count = lax.axis_size(axis)
    return lax.ppermute(array, axis, [(i, i ^ 1) for i in range(count)])


def along_pairs(array, by):
    half = lax.axis_size("ctx") // 2
    pairs = [
        (2 * i + r, (i + by) % half * 2 + r) for i in range(half) for r in range(2)
    ]
    return lax.ppermute(array, "ctx", pairs)


def barrier(*values):
    return lax.optimization_barrier(values)


def add(*parts):
    return sum(part.astype(F32) for part in parts)


def token_experts(expert_in, gates, up_weight, down_weight):
    half = lax.axis_size("ctx") // 2
    up_t = jnp.swapaxes(up_weight, 1, 2)
    turns = [0] + [s for s in (1, 3, 2) if 0 < s < half]
    turns = list(dict.fromkeys(turns))
    come = {0: expert_in}
    for s in turns[1:]:
        come[s] = along_pairs(expert_in, s)
    total = None
    held, block = None, None
    for s in turns:
        same = come[s]
        across = swap_axis(same, "ctx")
        blocks = [same, across, swap_axis(same, "exp"), swap_axis(across, "exp")]
        if held is not None:
            *blocks, _ = barrier(*blocks, held)
        near, far, near_out, far_out = dense_expert(blocks, gates[s], up_t, down_weight)
        far = add(far, swap_axis(far_out, "exp")).astype(BF16)
        held = far
        near = add(near, swap_axis(near_out, "exp"))
        if s == 0:
            home = near.astype(BF16), far
            continue
        block = add(near, swap_axis(far, "ctx")).astype(BF16)
        last = block
        block = along_pairs(block, -s)
        total = add(block) if total is None else add(total, block)
    near, far, _ = barrier(*home, last)
    return add(total, near, swap_axis(far, "ctx"))


def per_device(
    x_in,
    bc_in,
    z_in,
    time_step,
    decay_log,
    conv_inner,
    conv_bc,
    skip_gain,
    start_state,
    norm_gain,
    out_proj,
    residual,
    moe_gain,
    routes,
    gate_weight,
    up_weight,
    down_weight,
):
    ctx_count = lax.axis_size("ctx")
    exp_count = lax.axis_size("exp")
    exp_index = lax.axis_index("exp")
    block_len = x_in.shape[0]
    local_heads = time_step.shape[1]
    local_groups = bc_in.shape[2] // STATE
    per_group = local_heads // local_groups
    rim_rows = KERNEL - 1
    proj = lax.all_gather(out_proj.T, "ctx", axis=0, tiled=True)

    tok_rows = routes.shape[0]
    top_count = routes.shape[1]
    experts = ctx_count * exp_count * up_weight.shape[0]
    capacity = max(2, 4 * tok_rows * top_count // (3 * experts))
    chosen = routes[:, :, None] == jnp.arange(experts, dtype=jnp.int32)[None, None, :]
    dense_gate = jnp.sum(jnp.where(chosen, gate_weight[:, :, None], 0.0), axis=1)
    log_steps = decay_log.reshape(block_len, local_groups, per_group)
    cumulative = jnp.cumsum(log_steps, axis=0)
    block_log = cumulative[block_len - 1]
    table = jnp.concatenate(
        [dense_gate.T, jnp.pad(block_log.reshape(1, -1), ((0, 0), (0, tok_rows - local_heads)))], 0
    )
    tables = lax.all_gather(table, ("ctx", "exp"), axis=0)
    ctx_index = lax.axis_index("ctx")
    me = ctx_index * exp_count + exp_index
    gates = lax.dynamic_index_in_dim(tables, me, 1, False)
    logs = lax.dynamic_index_in_dim(
        tables[:, experts, :local_heads].reshape(ctx_count, exp_count, local_groups, per_group),
        exp_index,
        1,
        False,
    )
    member = gates > 0.0
    slots = jnp.where(member, jnp.cumsum(member.astype(jnp.int32), axis=1) - 1, -1)

    prev_inner, prev_bc = from_behind(
        (x_in[block_len - rim_rows :], bc_in[block_len - rim_rows :]), "ctx", 1
    )
    inner_act = causal_conv(x_in, prev_inner, conv_inner)
    bc_act = causal_conv(bc_in, prev_bc, conv_bc)
    values = inner_act.astype(F32).reshape(block_len, local_groups, per_group, HEAD_DIM)
    b_rows = bc_act[:, 0].astype(F32).reshape(block_len, local_groups, STATE)
    c_rows = bc_act[:, 1].astype(F32).reshape(block_len, local_groups, STATE)
    step_sizes = time_step.reshape(block_len, local_groups, per_group)
    to_end = jnp.exp(block_log[None] - cumulative) * step_sizes
    end_state = jnp.einsum("tgrp,tgn->grpn", to_end[..., None] * values, b_rows, precision=HIGH)
    entering = entering_state(
        block_log,
        logs,
        end_state,
        start_state.astype(F32).reshape(local_groups, per_group, HEAD_DIM, STATE),
    )
    carried = jnp.exp(cumulative)[..., None] * jnp.einsum(
        "tgn,grpn->tgrp", c_rows, entering, precision=HIGH
    )
    scores = jnp.einsum("tgn,sgn->tsg", c_rows, b_rows, precision=HIGH)
    position = jnp.arange(block_len)
    causal = (position[:, None] >= position[None, :])[:, :, None, None]
    spread_log = cumulative[:, None] - cumulative[None, :]
    decay_table = jnp.where(causal, jnp.exp(jnp.where(causal, spread_log, 0.0)), 0.0)
    mix_table = decay_table * step_sizes[None] * scores[..., None]
    local_part = jnp.einsum("tsgr,sgrp->tgrp", mix_table, values, precision=HIGH)
    outputs = (
        carried + local_part + skip_gain.reshape(local_groups, per_group)[None, :, :, None] * values
    )
    gated = outputs.reshape(block_len, local_groups, -1) * jax.nn.silu(
        z_in.astype(F32).reshape(block_len, local_groups, -1)
    )
    mean_square = jnp.mean(gated * gated, axis=-1, keepdims=True)
    normed = (
        (gated * lax.rsqrt(mean_square + EPS) * norm_gain.astype(F32).reshape(local_groups, -1))
        .reshape(block_len, -1)
        .astype(BF16)
    )

    def projected(part):
        rows = lax.dynamic_slice_in_dim(normed, part * tok_rows, tok_rows, 0)
        return lax.dot_general(rows, proj, (((1,), (1,)), ((), ())), preferred_element_type=F32)

    theirs = lax.ppermute(projected(1 - exp_index), "exp", [(0, 1), (1, 0)])
    mixed = projected(exp_index) + theirs
    hidden_f = (residual.astype(F32) + mixed).astype(BF16).astype(F32)
    expert_in = (
        hidden_f
        * lax.rsqrt(jnp.mean(hidden_f * hidden_f, axis=-1, keepdims=True) + EPS)
        * moe_gain.astype(F32)
    ).astype(BF16)
    half = ctx_count // 2
    if ctx_count % 2 == 0 and 1 < half <= 4 and exp_count == 2:
        shift, place = jnp.arange(half)[:, None], jnp.arange(4)[None, :]
        source = (
            (ctx_index // 2 - shift) % half * 4
            + (ctx_index + place) % 2 * 2
            + (exp_index + place // 2) % 2
        )
        combined = token_experts(
            expert_in, gates[source].reshape(half, -1, 1), up_weight, down_weight
        )
    else:
        tokens = lax.all_gather(expert_in, ("ctx", "exp"), axis=0, tiled=True)
        answers = run_expert(tokens, slots, gates, up_weight, down_weight, capacity)
        combined = lax.psum_scatter(answers, ("ctx", "exp"), scatter_dimension=0, tiled=True)
    return (hidden_f + combined.astype(F32)).astype(BF16)


def solution(mesh):
    in_specs = (
        P(("groups", "ctx"), "exp"),
        P(("groups", "ctx"), None, "exp"),
        P(("groups", "ctx"), "exp"),
        P(("groups", "ctx"), "exp"),
        P(("groups", "ctx"), "exp"),
        P(None, "exp"),
        P(None, None, "exp"),
        P("exp"),
        P(("groups", "exp"), None, None),
        P("exp"),
        P("exp", "ctx"),
        P(("groups", "ctx", "exp"), None),
        P(),
        P(("groups", "ctx", "exp"), None),
        P(("groups", "ctx", "exp"), None),
        P(("ctx", "exp"), None, None),
        P(("ctx", "exp"), None, None),
    )
    out_specs = P(("groups", "ctx", "exp"), None)
    return jax.shard_map(
        per_device, mesh=mesh, in_specs=in_specs, out_specs=out_specs, check_vma=False
    )
```
